32 devices in a mesh: dp: 2 (over x), seq: 16 (over z, y, core).
Axes of the slice: x: 2, y: 2, z: 4, core: 2. Of those that a mesh axis runs over, the one named last changes fastest.
Arguments:
- queries: bfloat16 [4096, 1024], P(('dp', 'seq')), parts along dimension 0, may hold values from -6 to 6
- keys: bfloat16 [4096, 1024], P(('dp', 'seq')), parts along dimension 0, may hold values from -6 to 6
- values: bfloat16 [4096, 1024], P(('dp', 'seq')), parts along dimension 0, may hold values from -36 to 36
- feat_weight: bfloat16 [16, 64, 256], replicated, may hold values from -0.75 to 0.75
- norm_gain: bfloat16 [1024], replicated, may hold values from 0.25 to 1.75
- counts: int32 [32, 16], P('dp'), parts along dimension 0, may hold values from 4 to 12, as said below
- offsets: int32 [32, 16], P('dp'), parts along dimension 0, may hold values from 0 to 127, as said below
Outputs:
- mixed: bfloat16 [4096, 1024], P(('dp', 'seq')), parts along dimension 0
The draws below stay inside these ranges and needn't reach their ends.
There are 2 independent parts, one for each index of `dp`. The reference program is written for one: setup_inputs(seed, part) draws one part's arguments, and reference() takes and returns one part's arrays. A program takes and returns all parts, laid end to end along the dimension named above; an argument that names none is the same for every part. Nothing has to cross between parts.
Inputs may be any that keep to these rules, and one draw needn't show every extreme that they name: Each row and each column of counts sums to 128; every loader sends 12 rows to exactly one device. For each device d the ranges from offsets[j, d] to offsets[j, d] + counts[j, d] - 1 over all loaders j tile 0 to 127.
All inputs are finite; a program needn't handle non-finite values.
Results may differ from the reference program's by a relative error of at most 0.0023.
Values may be sent and summed in bfloat16 or wider, within the bound.
A program may use at most 192 MiB of HBM per device.

```python
import jax
import jax.numpy as jnp
from jax import lax

HEADS = 16
HEAD = 64
FEAT = 256
VDIM = 64
TOK_DEV = 128
TOKENS = 2048
BASE = 8
SPREAD = 4
N_SEQ = 16


def route_tables(key):
    table_key = jax.random.fold_in(key, 7)
    first_key, second_key, third_key = jax.random.split(table_key, 3)
    sigma = jax.random.permutation(first_key, N_SEQ).astype(jnp.int32)
    shifts = jax.random.randint(second_key, (SPREAD,), 1, N_SEQ).astype(jnp.int32)
    loaders = jnp.arange(N_SEQ, dtype=jnp.int32)
    peak = (loaders[None, :] == sigma[:, None]).astype(jnp.int32)
    taken_index = sigma[(loaders[None, :] + shifts[:, None]) % N_SEQ]
    taken = jnp.sum((taken_index[:, :, None] == loaders[None, None, :]).astype(jnp.int32), axis=0)
    counts = (BASE + SPREAD * peak - taken).astype(jnp.int32)
    order_keys = jax.random.split(third_key, N_SEQ)
    ranks = jax.vmap(lambda one_key: jax.random.permutation(one_key, N_SEQ))(order_keys).T.astype(jnp.int32)
    before = (ranks[None, :, :] < ranks[:, None, :]).astype(jnp.int32)
    offsets = jnp.sum(before * counts[None, :, :], axis=1).astype(jnp.int32)
    return (counts, offsets)


def draw_counts(key, part):
    return route_tables(key)[0]


def draw_offsets(key, part):
    return route_tables(key)[1]


def draw_values(key, part):
    value_key = jax.random.fold_in(key, 11)
    base_key, row_key, column_key = jax.random.split(value_key, 3)
    row_scale = jnp.exp(jax.random.uniform(row_key, (TOKENS, 1), jnp.float32, jnp.log(0.3), jnp.log(3.0)))
    column_scale = jnp.exp(jax.random.uniform(column_key, (1, HEADS * VDIM), jnp.float32, jnp.log(0.3), jnp.log(3.0)))
    basic = jnp.clip(jax.random.normal(base_key, (TOKENS, HEADS * VDIM), jnp.float32), -4.0, 4.0)
    return (basic * row_scale * column_scale).astype(jnp.bfloat16)


def steps_of(key, dims, cuts, least, largest):
    loudness = 1.0
    for dim, shards_of in cuts:
        draws = jax.random.uniform(jax.random.fold_in(jax.random.fold_in(key, 6), dim), (shards_of,), jnp.float32, least / len(cuts), largest / len(cuts))
        loudness = loudness * jnp.repeat(jnp.exp(draws), dims[dim] // shards_of).reshape((-1,) + (1,) * (len(dims) - 1 - dim))
    return loudness


def normal_values(stream_key, dims, spread, most, cuts=(), kind=jnp.bfloat16):
    level = steps_of(stream_key, dims, cuts, -0.22, 0.18) if cuts else 1.0
    entries = jax.random.normal(stream_key, dims, jnp.float32) * spread * level
    return jnp.minimum(jnp.maximum(entries, -most), most).astype(kind)


def setup_inputs(seed: int = 0, part: int = 0) -> dict:
    key_of = jax.random.split(jax.random.key(seed), 8)
    part_keys = jax.random.split(jax.random.fold_in(key_of[7], part), 8)
    queries = normal_values(part_keys[0], (TOKENS, HEADS * HEAD), 1.0, 6.0, ((0, 16),))
    keys = normal_values(part_keys[1], (TOKENS, HEADS * HEAD), 1.0, 6.0, ((0, 16),))
    values = draw_values(jax.random.fold_in(jax.random.fold_in(key_of[7], part), 71), part)
    feat_weight = normal_values(key_of[3], (HEADS, HEAD, FEAT), HEAD ** -0.5, 0.75)
    norm_gain = jnp.clip(1.0 + 0.15 * jax.random.normal(key_of[4], (HEADS * VDIM,), jnp.float32), 0.25, 1.75).astype(jnp.bfloat16)
    counts = draw_counts(jax.random.fold_in(jax.random.fold_in(key_of[7], part), 71), part)
    offsets = draw_offsets(jax.random.fold_in(jax.random.fold_in(key_of[7], part), 71), part)
    return {"queries": queries, "keys": keys, "values": values, "feat_weight": feat_weight, "norm_gain": norm_gain, "counts": counts, "offsets": offsets}


def trace_positions(counts, offsets):
    starts = (jnp.cumsum(counts, axis=1) - counts).astype(jnp.int32)
    inner = jnp.arange(TOK_DEV, dtype=jnp.int32)
    device_ids = jnp.arange(N_SEQ, dtype=jnp.int32)

    def one_loader(start_row, count_row, offset_row):
        inside = (inner[:, None] >= start_row[None, :]) & (inner[:, None] < (start_row + count_row)[None, :])
        hot = inside.astype(jnp.int32)
        target = lax.optimization_barrier(jnp.sum(hot * device_ids[None, :], axis=1)).astype(jnp.int32)
        shift = lax.optimization_barrier(jnp.sum(hot * (offset_row - start_row)[None, :], axis=1)).astype(jnp.int32)
        return (target * TOK_DEV + shift + inner).astype(jnp.int32)
    return jax.vmap(one_loader)(starts, counts, offsets).reshape(-1)

def feature_map(rows, feat_weight):
    split_rows = rows.reshape(rows.shape[0], HEADS, HEAD).astype(jnp.float32)
    projected = jnp.einsum('thd,hdf->htf', split_rows, feat_weight.astype(jnp.float32), precision=lax.Precision.HIGHEST)
    return (jax.nn.elu(projected) + 1.0).astype(jnp.bfloat16)

def reference(queries, keys, values, feat_weight, norm_gain, counts, offsets):
    position = trace_positions(counts, offsets)
    packed_q = jnp.zeros(queries.shape, queries.dtype).at[position].set(queries)
    packed_k = jnp.zeros(keys.shape, keys.dtype).at[position].set(keys)
    packed_v = jnp.zeros(values.shape, values.dtype).at[position].set(values)
    inner = jnp.arange(TOK_DEV, dtype=jnp.int32)
    causal = inner[:, None] >= inner[None, :]
    gain = norm_gain.astype(jnp.float32).reshape(HEADS, 1, VDIM)

    def block_step(state, block):
        block_q, block_k, block_v = block
        phi_query = feature_map(block_q, feat_weight).astype(jnp.float32)
        phi_key = feature_map(block_k, feat_weight).astype(jnp.float32)
        value_heads = block_v.reshape(TOK_DEV, HEADS, VDIM).transpose(1, 0, 2).astype(jnp.float32)
        scores = jnp.einsum('hsf,htf->hst', phi_query, phi_key, precision=lax.Precision.HIGHEST)
        scores = jnp.where(causal[None, :, :], scores, 0.0)
        attended = jnp.einsum('hst,htv->hsv', scores, value_heads, precision=lax.Precision.HIGHEST)
        attended = attended + jnp.einsum('hsf,hfv->hsv', phi_query, state, precision=lax.Precision.HIGHEST)
        state = state + jnp.einsum('htf,htv->hfv', phi_key, value_heads, precision=lax.Precision.HIGHEST)
        centre = lax.optimization_barrier(jnp.mean(attended, axis=2, keepdims=True))
        centred = attended - centre
        spread_sq = lax.optimization_barrier(jnp.mean(centred * centred, axis=2, keepdims=True))
        normed = centred * lax.rsqrt(spread_sq + 1e-05) * gain
        return (state, normed.transpose(1, 0, 2).reshape(TOK_DEV, HEADS * VDIM).astype(jnp.bfloat16))
    blocks = (packed_q.reshape(N_SEQ, TOK_DEV, -1), packed_k.reshape(N_SEQ, TOK_DEV, -1), packed_v.reshape(N_SEQ, TOK_DEV, -1))
    initial = jnp.zeros((HEADS, FEAT, VDIM), jnp.float32)
    final_state, normed_blocks = lax.scan(block_step, initial, blocks)
    normed = normed_blocks.reshape(TOKENS, HEADS * VDIM)
    return normed[position]
```

```python
import functools

import jax
import jax.numpy as jnp
from jax import lax
from jax.experimental import pallas as pl
from jax.experimental.pallas import tpu as pltpu
from jax.sharding import PartitionSpec as P

MESH = pl.DeviceIdType.MESH
F32 = jnp.float32
BF16 = jnp.bfloat16
GROUPS = 4
TILE = 16


def block_bounds(n, rows, i):
    least = rows // n // 2
    most = 3 * (rows // n) // 2
    first = min(d for d in range(n) if min(most * (d + 1), rows - least * (n - d - 1)) > i)
    last = max(d for d in range(n) if max(least * d, rows - most * (n - d)) <= i)
    return first, last


def kernel(
    n,
    parts,
    returns,
    q_ref,
    k_ref,
    v_ref,
    w_ref,
    gain_ref,
    counts_ref,
    offsets_ref,
    out_ref,
    q_buf,
    k_buf,
    v_buf,
    w_buf,
    gain_buf,
    counts_buf,
    offsets_buf,
    load_sem,
    send,
    recv,
    phi_q,
    phi_kt,
    val,
    post,
    slot_row,
    slot_col,
    state,
    wq,
    wkt,
    out_send,
    out_recv,
    send_sem,
    recv_sem,
    back_send_sem,
    back_recv_sem,
    stage_sem,
):
    rows = q_ref.shape[0]
    width = q_ref.shape[1] // n
    tiles = rows // TILE
    tokens = n * TILE
    me = lax.axis_index("seq")

    bounds = [
        (block_bounds(n, rows, TILE * a)[0], block_bounds(n, rows, TILE * a + TILE - 1)[1])
        for a in range(tiles)
    ]
    full = [sum(1 for b in range(tiles) if bounds[b][1] < bounds[a][0]) for a in range(tiles)]
    ends = [sum(1 for b in range(tiles) if bounds[b][0] <= bounds[a][1]) for a in range(tiles)]

    half = n // 2
    own = me // half * half

    def near(dev):
        return lax.rem(dev + n - own, n)

    def near_for(peer):
        return lax.rem(me + n - peer // half * half, n)

    loads = [
        pltpu.make_async_copy(src, dst, load_sem.at[i])
        for i, (src, dst) in enumerate(
            (
                (q_ref, q_buf),
                (k_ref, k_buf),
                (v_ref, v_buf),
                (counts_ref, counts_buf),
                (offsets_ref, offsets_buf),
                (w_ref.at[me], w_buf),
                (gain_ref, gain_buf),
            )
        )
    ]
    for load in loads:
        load.start()

    def hops(peer):
        across = jnp.abs(peer // 4 - me // 4)
        return across + jnp.abs(peer // 2 % 2 - me // 2 % 2)

    def each(order, do):
        def body(step, carry):
            do(order(step))
            return carry

        lax.fori_loop(1, n, body, 0)

    def swap(step):
        return me ^ step

    def ahead(step):
        return lax.rem(me + step, n)

    def behind(step):
        return lax.rem(me + n - step, n)

    def tell(sem, reach):
        def one(peer):
            @pl.when(hops(peer) <= reach)
            def _():
                pl.semaphore_signal(sem, inc=1, device_id={"seq": peer}, device_id_type=MESH)

        each(swap, one)

    def within(reach):
        return sum(jnp.where(hops(me ^ step) <= reach, 1, 0) for step in range(1, n))

    stages = [1, 1, max(n // 4 - 2, 1)]
    barrier = pltpu.get_barrier_semaphore()
    tell(barrier, stages[0])

    for load in loads[:3]:
        load.wait()

    starts = []
    at = 0
    for first, last in parts:
        starts.append((at, at + (last - first) * TILE, at + (last - first) * (TILE + TILE // 2)))
        at = starts[-1][2]

    for pair in range(n // 2):
        lanes = slice(2 * width * pair, 2 * width * (pair + 1))
        q = q_buf[:, lanes]
        k = k_buf[:, lanes]
        v = v_buf[:, lanes]
        for (first, last), (base, mid, end) in zip(parts, starts):
            here = slice(first * TILE, last * TILE)
            send[2 * pair, base:mid, :] = jnp.concatenate([q[here, :width], k[here, :width]], axis=1)
            send[2 * pair + 1, base:mid, :] = jnp.concatenate([q[here, width:], k[here, width:]], axis=1)
            for a in range(first, last, 2):
                to = slice(mid + (a - first) * TILE // 2, mid + (a - first + 2) * TILE // 2)
                even = v[a * TILE : (a + 1) * TILE]
                odd = v[(a + 1) * TILE : (a + 2) * TILE]
                send[2 * pair, to, :] = jnp.concatenate([even[:, :width], odd[:, :width]], axis=1)
                send[2 * pair + 1, to, :] = jnp.concatenate([even[:, width:], odd[:, width:]], axis=1)

    def forward(peer, g):
        piece = slice(starts[g][0], starts[g][2])
        return pltpu.make_async_remote_copy(
            src_ref=send.at[peer, piece],
            dst_ref=recv.at[near_for(peer), piece],
            send_sem=send_sem.at[peer, g],
            recv_sem=recv_sem.at[me, g],
            device_id={"seq": peer},
            device_id_type=MESH,
        )

    def arrive(src, g):
        piece = slice(starts[g][0], starts[g][2])
        pltpu.make_async_remote_copy(
            src_ref=send.at[src, piece],
            dst_ref=recv.at[near(src), piece],
            send_sem=send_sem.at[src, g],
            recv_sem=recv_sem.at[src, g],
            device_id={"seq": src},
            device_id_type=MESH,
        ).wait_recv()

    def send_between(low, high):
        def one(peer):
            @pl.when((hops(peer) > low) & (hops(peer) <= high))
            def _():
                forward(peer, 0).start()

        each(swap, one)

    pl.semaphore_wait(barrier, within(stages[0]))
    tell(stage_sem.at[0], stages[1])
    send_between(-1, stages[0])
    recv[near(me)] = send[me]

    for load in loads[3:]:
        load.wait()
    lane = lax.broadcasted_iota(jnp.int32, (n, rows), 1)
    start = jnp.zeros((n, 1), jnp.int32)
    position = lane
    for d in range(n):
        count = counts_buf[:, d : d + 1]
        inside = (lane >= start) & (lane < start + count)
        position = position + jnp.where(inside, d * rows + offsets_buf[:, d : d + 1] - start, 0)
        start = start + count
    position = position.astype(F32)

    pl.semaphore_wait(stage_sem.at[0], within(stages[1]))
    tell(stage_sem.at[1], stages[2])
    send_between(stages[0], stages[0] + stages[1])

    if n < rows:
        position = jnp.concatenate([position, jnp.zeros((rows - n, rows), F32)], axis=0)
    post[...] = position.T

    pl.semaphore_wait(stage_sem.at[1], within(stages[2]))
    send_between(stages[0] + stages[1], n)
    for g in range(1, len(parts)):
        each(ahead, lambda peer: forward(peer, g).start())

    for j in range(n):
        column = jnp.broadcast_to(post[:, j : j + 1], (rows, 128))
        slot_col[:, near(j)] = column.reshape(tiles, TILE, 128)
    for a in range(tiles):
        slot_row[a] = slot_col[a].reshape(tokens, 128).T[0:8, :]

    w = w_buf[...]
    blank = jnp.zeros_like(w)
    wq[...] = jnp.concatenate([w, blank], axis=0)
    wkt[...] = jnp.concatenate([blank, w], axis=0).astype(F32).T.astype(BF16)
    gains = gain_buf[...].astype(F32).reshape(1, n * width)
    gain = jnp.zeros((1, width), F32)
    for h in range(n):
        gain = gain + jnp.where(me == h, gains[:, h * width : (h + 1) * width], 0.0)

    def feature(z):
        return jnp.where(z > 0.0, z + 1.0, jnp.exp(jnp.minimum(z, 0.0))).astype(BF16)

    share = tokens // 2

    def take(a, part):
        g = next(i for i, (first, last) in enumerate(parts) if first <= a < last)
        first = parts[g][0]
        base, mid, _ = starts[g]
        here = slice(base + (a - first) * TILE, base + (a - first + 1) * TILE)
        group = slice(part * half, (part + 1) * half)
        slots = slice(a * tokens + part * share, a * tokens + (part + 1) * share)
        x = recv[group, here, :].reshape(share, 2 * width)
        phi_q[slots, :] = feature(jnp.dot(x, wq[...], preferred_element_type=F32))
        keys = lax.dot_general(wkt[...], x, (((1,), (1,)), ((), ())), preferred_element_type=F32)
        phi_kt[:, slots] = feature(keys)
        there = mid + (a - first) // 2 * TILE
        v = recv[group, there : there + TILE, :].reshape(share, 2 * width)
        val[slots, :] = v[:, width:] if a % 2 else v[:, :width]

    def tile(a, count, b0, b1):
        size = count * tokens
        span = (b1 - b0) * tokens
        scores = jnp.dot(
            phi_q[a * tokens : a * tokens + size, :],
            phi_kt[:, b0 * tokens : b1 * tokens],
            preferred_element_type=F32,
        )
        later = slot_col[a : a + count].reshape(size // 8, 8, 128)
        later = jnp.concatenate([later] * (span // 128), axis=2)
        earlier = jnp.concatenate([slot_row[b] for b in range(b0, b1)], axis=1)
        keep = earlier[None] <= later
        scores = jnp.where(keep, scores.reshape(size // 8, 8, span), 0.0).reshape(size, span)
        high = scores.astype(BF16)
        low = (scores - high.astype(F32)).astype(BF16)
        both = jnp.dot(
            jnp.concatenate([high, low], axis=0),
            val[b0 * tokens : b1 * tokens, :],
            preferred_element_type=F32,
        )
        return both[:size] + both[size:]

    marks = sorted(set(f for f in full if f))

    sums = []

    def add_state():
        b0 = marks[len(sums) - 1] if sums else 0
        b1 = marks[len(sums)]
        total = jnp.dot(
            phi_kt[:, b0 * tokens : b1 * tokens],
            val[b0 * tokens : b1 * tokens, :],
            preferred_element_type=F32,
        )
        if sums:
            total = sums[-1] + total
        high = total.astype(BF16)
        low = (total - high.astype(F32)).astype(BF16)
        state[len(sums)] = jnp.concatenate([high, low], axis=1)
        sums.append(total)

    def from_state(a):
        while len(sums) <= marks.index(full[a]):
            add_state()
        both = jnp.dot(
            phi_q[a * tokens : (a + 1) * tokens, :], state[marks.index(full[a])], preferred_element_type=F32
        )
        return both[:, :width] + both[:, width:]

    def sweep(a, count, b0, b1, step):
        total = None
        for b in range(b0, b1, step):
            piece = tile(a, count, b, min(b + step, b1))
            total = piece if total is None else total + piece
        return total

    def attend(a):
        b0, b1 = full[a + 1], ends[a]
        shared = sweep(a, 2, b0, b1, 2)
        totals = [shared[:tokens], shared[tokens:]]
        for i, (c0, c1) in enumerate(((full[a], b0), (b1, ends[a + 1]))):
            if c0 < c1:
                totals[i] = totals[i] + sweep(a + i, 1, c0, c1, 3)
            if full[a + i]:
                totals[i] = totals[i] + from_state(a + i)
        return totals

    def normalise(attended):
        centre = jnp.mean(attended, axis=1, keepdims=True)
        centred = attended - centre
        spread = jnp.mean(centred * centred, axis=1, keepdims=True)
        return (centred * lax.rsqrt(spread + 1e-05) * gain).astype(BF16)

    def pack(a, even, odd):
        y = jnp.concatenate([even, odd], axis=1).reshape(n, TILE, 2 * width)
        out_send[:, a * TILE // 2 : a * TILE // 2 + TILE, :] = y

    def piece_of(g):
        return slice(returns[g][0] * TILE // 2, returns[g][1] * TILE // 2)

    def back(loader, g):
        return pltpu.make_async_remote_copy(
            src_ref=out_send.at[near(loader), piece_of(g)],
            dst_ref=out_recv.at[me, piece_of(g)],
            send_sem=back_send_sem.at[loader, g],
            recv_sem=back_recv_sem.at[me, g],
            device_id={"seq": loader},
            device_id_type=MESH,
        )

    def collect(src, g):
        pltpu.make_async_remote_copy(
            src_ref=out_send.at[src, piece_of(g)],
            dst_ref=out_recv.at[src, piece_of(g)],
            send_sem=back_send_sem.at[src, g],
            recv_sem=back_recv_sem.at[src, g],
            device_id={"seq": src},
            device_id_type=MESH,
        ).wait_recv()

    for g, (first, last) in enumerate(parts):
        for step in range(1, half):
            arrive(own + lax.rem(me + step, half), g)
        for a in range(first, last):
            take(a, 0)

    sent = 0
    ready = 0
    for a in range(0, tiles, 2):
        for g, (first, last) in enumerate(parts):
            if ready <= first < ends[a + 1]:
                lax.fori_loop(0, half, lambda i, c: (arrive(lax.rem(own + half + i, n), g), c)[1], 0)
                for b in range(first, last):
                    take(b, 1)
                ready = last
        pack(a, *(normalise(total) for total in attend(a)))
        while sent < len(returns) and returns[sent][1] <= a + 2:
            each(ahead, lambda loader: back(loader, sent).start())
            sent += 1
        while len(sums) < len(marks) and marks[len(sums)] <= ready:
            add_state()

    out_recv[me] = out_send[near(me)]
    for g, (first, last) in enumerate(returns):
        each(behind, lambda src: collect(src, g))
        for a in range(first, last, 2):
            here = slice(a * TILE // 2, a * TILE // 2 + TILE)
            for pair in range(n // 2):
                lanes = slice(2 * width * pair, 2 * width * (pair + 1))
                x = out_recv[2 * pair, here, :]
                y = out_recv[2 * pair + 1, here, :]
                out_ref[a * TILE : (a + 1) * TILE, lanes] = jnp.concatenate(
                    [x[:, :width], y[:, :width]], axis=1
                )
                out_ref[(a + 1) * TILE : (a + 2) * TILE, lanes] = jnp.concatenate(
                    [x[:, width:], y[:, width:]], axis=1
                )

    def drain(peer):
        for g in range(len(parts)):
            forward(peer, g).wait_send()
        for g in range(len(returns)):
            back(peer, g).wait_send()

    each(ahead, drain)


def grouped_kernel(
    n,
    heads,
    q_ref,
    k_ref,
    v_ref,
    w_ref,
    gain_ref,
    counts_ref,
    offsets_ref,
    out_ref,
    q_buf,
    k_buf,
    v_buf,
    w_buf,
    gain_buf,
    counts_buf,
    offsets_buf,
    load_sem,
    send,
    recv,
    phi_q,
    phi_kt,
    val,
    posr,
    post,
    posc,
    slot_row,
    slot_col,
    acc,
    wq,
    wkt,
    out_send,
    out_recv,
    send_sem,
    recv_sem,
    back_send_sem,
    back_recv_sem,
):
    rows = q_ref.shape[0]
    half = rows // 2
    width = q_ref.shape[1] // heads
    feat = w_ref.shape[2]
    group = n // heads
    part_rows = rows // group
    part_half = part_rows // 2
    total = n * rows
    queries = n * part_rows
    me = lax.axis_index("seq")
    head = me // group
    part = me % group

    half_ring = n // 2
    own = me // half_ring * half_ring
    other = lax.rem(own + half_ring, n)

    def target(step):
        return jnp.where(step < half_ring, own, other) + lax.rem(me + step, half_ring)

    def source(step):
        return jnp.where(step < half_ring, own, other) + lax.rem(me + n - step, half_ring)

    loads = [
        pltpu.make_async_copy(src, dst, load_sem.at[i])
        for i, (src, dst) in enumerate(
            (
                (q_ref, q_buf),
                (k_ref, k_buf),
                (v_ref, v_buf),
                (counts_ref, counts_buf),
                (offsets_ref, offsets_buf),
                (w_ref.at[head], w_buf),
                (gain_ref, gain_buf),
            )
        )
    ]
    for load in loads:
        load.start()

    barrier = pltpu.get_barrier_semaphore()

    def greet(step, carry):
        peer = lax.rem(me + step, n)
        pl.semaphore_signal(barrier, inc=1, device_id={"seq": peer}, device_id_type=MESH)
        return carry

    lax.fori_loop(1, n, greet, 0)

    for load in loads[:3]:
        load.wait()

    for pair in range(heads // 2):
        lanes = slice(2 * width * pair, 2 * width * (pair + 1))
        q = q_buf[:, lanes]
        k = k_buf[:, lanes]
        v = v_buf[:, lanes]
        send[2 * pair, 0:rows, :] = jnp.concatenate([q[:, :width], k[:, :width]], axis=1)
        send[2 * pair + 1, 0:rows, :] = jnp.concatenate([q[:, width:], k[:, width:]], axis=1)
        send[2 * pair, rows:, :] = jnp.concatenate([v[:half, :width], v[half:, :width]], axis=1)
        send[2 * pair + 1, rows:, :] = jnp.concatenate([v[:half, width:], v[half:, width:]], axis=1)

    pl.semaphore_wait(barrier, n - 1)

    def forward(peer):
        return pltpu.make_async_remote_copy(
            src_ref=send.at[peer // group],
            dst_ref=recv.at[me],
            send_sem=send_sem.at[peer],
            recv_sem=recv_sem.at[me],
            device_id={"seq": peer},
            device_id_type=MESH,
        )

    def send_one(step, carry):
        forward(target(step)).start()
        return carry

    lax.fori_loop(1, n, send_one, 0)
    recv[me] = send[head]

    for load in loads[3:]:
        load.wait()

    lane = lax.broadcasted_iota(jnp.int32, (n, rows), 1)
    start = jnp.zeros((n, 1), jnp.int32)
    position = lane
    for d in range(n):
        count = counts_buf[:, d : d + 1]
        inside = (lane >= start) & (lane < start + count)
        position = position + jnp.where(inside, d * rows + offsets_buf[:, d : d + 1] - start, 0)
        start = start + count
    position = position.astype(F32)
    posr[...] = position
    if n < rows:
        position = jnp.concatenate([position, jnp.zeros((rows - n, rows), F32)], axis=0)
    post[...] = position.T
    mine = post[pl.ds(pl.multiple_of(part * part_rows, part_rows), part_rows), :]
    for j in range(n):
        posc[j * part_rows : (j + 1) * part_rows, :] = jnp.broadcast_to(
            mine[:, j : j + 1], (part_rows, 128)
        )

    w = w_buf[...]
    blank = jnp.zeros_like(w)
    wq[...] = jnp.concatenate([w, blank], axis=0)
    wkt[...] = jnp.concatenate([blank, w], axis=0).astype(F32).T.astype(BF16)
    gain = jnp.zeros((1, width), F32)
    for h in range(heads):
        gain = gain + jnp.where(head == h, gain_buf[:, h * width : (h + 1) * width].astype(F32), 0.0)

    def feature(z):
        return jnp.where(z > 0.0, z + 1.0, jnp.exp(jnp.minimum(z, 0.0))).astype(BF16)

    def take_block(step):
        src = source(step)
        x = recv[src, 0:rows, :]
        keys = lax.dot_general(wkt[...], x, (((1,), (1,)), ((), ())), preferred_element_type=F32)
        phi_kt[:, step * rows : (step + 1) * rows] = feature(keys)
        mine_of = pl.multiple_of(part * part_rows, part_rows)
        proj = jnp.dot(
            recv[src, pl.ds(mine_of, part_rows), :], wq[...], preferred_element_type=F32
        )
        slots = slice(step * part_rows, (step + 1) * part_rows)
        phi_q[slots, :] = feature(proj)
        block = recv[src, rows:, :]
        val[step * rows : step * rows + half, :] = block[:, :width]
        val[step * rows + half : (step + 1) * rows, :] = block[:, width:]
        slot_row[step : step + 1, :] = posr[pl.ds(src, 1), :]
        slot_col[slots, :] = posc[
            pl.ds(pl.multiple_of(src * part_rows, part_rows), part_rows), :
        ]

    def arrive(step):
        src = source(step)
        pltpu.make_async_remote_copy(
            src_ref=send.at[0],
            dst_ref=recv.at[src],
            send_sem=send_sem.at[src],
            recv_sem=recv_sem.at[src],
            device_id={"seq": src},
            device_id_type=MESH,
        ).wait_recv()

    groups = min(GROUPS, n)
    per = n // groups
    tile_r = per * part_rows
    tile_s = per * rows

    def tile(rb, sb):
        r0 = pl.multiple_of(rb * tile_r, tile_r)
        s0 = pl.multiple_of(sb * tile_s, tile_s)
        scores = jnp.dot(
            phi_q[pl.ds(r0, tile_r), :], phi_kt[:, pl.ds(s0, tile_s)], preferred_element_type=F32
        )
        later = jnp.concatenate([slot_col[pl.ds(r0, tile_r), :]] * per, axis=1)
        earlier = jnp.concatenate([slot_row[pl.ds(sb * per + i, 1), :] for i in range(per)], axis=1)
        scores = jnp.where(earlier <= later, scores, 0.0)
        high = scores.astype(BF16)
        low = (scores - high.astype(F32)).astype(BF16)
        vals = val[pl.ds(s0, tile_s), :]
        return jnp.dot(high, vals, preferred_element_type=F32) + jnp.dot(
            low, vals, preferred_element_type=F32
        )

    def back(step):
        loader = source(step)
        return pltpu.make_async_remote_copy(
            src_ref=out_send.at[step],
            dst_ref=out_recv.at[me],
            send_sem=back_send_sem.at[loader],
            recv_sem=back_recv_sem.at[me],
            device_id={"seq": loader},
            device_id_type=MESH,
        )

    def finish(rb, attended):
        centre = jnp.mean(attended, axis=1, keepdims=True)
        centred = attended - centre
        spread = jnp.mean(centred * centred, axis=1, keepdims=True)
        normed = (centred * lax.rsqrt(spread + 1e-05) * gain).astype(BF16)
        for i in range(per):
            y = normed[i * part_rows : (i + 1) * part_rows]
            out_send[rb * per + i] = jnp.concatenate([y[:part_half], y[part_half:]], axis=1)
        for i in range(per):
            if rb * per + i > 0:
                back(rb * per + i).start()

    def rows_of(rb):
        return pl.ds(pl.multiple_of(rb * tile_r, tile_r), tile_r)

    for gi in range(groups):
        for step in range(gi * per, (gi + 1) * per):
            if step > 0:
                arrive(step)
            take_block(step)
        last = gi == groups - 1
        fresh = tile(gi, gi)
        if not last:

            def both(i, fresh):
                acc[rows_of(i), :] = acc[rows_of(i), :] + tile(i, gi)
                return fresh + tile(gi, i)

            acc[rows_of(gi), :] = lax.fori_loop(0, gi, both, fresh)
        else:
            finish(gi, lax.fori_loop(0, gi, lambda i, fresh: fresh + tile(gi, i), fresh))
            for i in reversed(range(gi)):
                finish(i, acc[rows_of(i), :] + tile(i, gi))
    out_recv[me] = out_send[0]

    def collect(step, carry):
        src = source(step)
        pltpu.make_async_remote_copy(
            src_ref=out_send.at[step],
            dst_ref=out_recv.at[src],
            send_sem=back_send_sem.at[src],
            recv_sem=back_recv_sem.at[src],
            device_id={"seq": src},
            device_id_type=MESH,
        ).wait_recv()
        return carry

    lax.fori_loop(1, n, collect, 0)

    for piece in range(group):
        first = slice(piece * part_rows, piece * part_rows + part_half)
        second = slice(piece * part_rows + part_half, (piece + 1) * part_rows)
        for pair in range(heads // 2):
            lanes = slice(2 * width * pair, 2 * width * (pair + 1))
            a = out_recv[2 * pair * group + piece]
            b = out_recv[(2 * pair + 1) * group + piece]
            out_ref[first, lanes] = jnp.concatenate([a[:, :width], b[:, :width]], axis=1)
            out_ref[second, lanes] = jnp.concatenate([a[:, width:], b[:, width:]], axis=1)

    def drain(step, carry):
        peer = target(step)
        forward(peer).wait_send()
        back(step).wait_send()
        return carry

    lax.fori_loop(1, n, drain, 0)


def grouped(n, queries, keys, values, feat_weight, norm_gain, counts, offsets):
    rows = queries.shape[0]
    heads, width, feat = feat_weight.shape
    group = n // heads
    part_rows = rows // group
    total = n * rows
    lanes = 2 * width
    return pl.pallas_call(
        functools.partial(grouped_kernel, n, heads),
        out_shape=jax.ShapeDtypeStruct(queries.shape, BF16),
        in_specs=[pl.BlockSpec(memory_space=pltpu.HBM)] * 7,
        out_specs=pl.BlockSpec(memory_space=pltpu.VMEM),
        scratch_shapes=[
            pltpu.VMEM(queries.shape, BF16),
            pltpu.VMEM(keys.shape, BF16),
            pltpu.VMEM(values.shape, BF16),
            pltpu.VMEM((width, feat), BF16),
            pltpu.VMEM((1, norm_gain.shape[0]), BF16),
            pltpu.VMEM(counts.shape, jnp.int32),
            pltpu.VMEM(offsets.shape, jnp.int32),
            pltpu.SemaphoreType.DMA((7,)),
            pltpu.VMEM((heads, rows + rows // 2, lanes), BF16),
            pltpu.VMEM((n, rows + rows // 2, lanes), BF16),
            pltpu.VMEM((n * part_rows, feat), BF16),
            pltpu.VMEM((feat, total), BF16),
            pltpu.VMEM((total, width), BF16),
            pltpu.VMEM((n, rows), F32),
            pltpu.VMEM((rows, max(n, rows)), F32),
            pltpu.VMEM((n * part_rows, 128), F32),
            pltpu.VMEM((n, rows), F32),
            pltpu.VMEM((n * part_rows, 128), F32),
            pltpu.VMEM((n * part_rows, width), F32),
            pltpu.VMEM((lanes, feat), BF16),
            pltpu.VMEM((feat, lanes), BF16),
            pltpu.VMEM((n, part_rows // 2, lanes), BF16),
            pltpu.VMEM((n, part_rows // 2, lanes), BF16),
            pltpu.SemaphoreType.DMA((n,)),
            pltpu.SemaphoreType.DMA((n,)),
            pltpu.SemaphoreType.DMA((n,)),
            pltpu.SemaphoreType.DMA((n,)),
        ],
        compiler_params=pltpu.CompilerParams(
            collective_id=0, has_side_effects=True, vmem_limit_bytes=67043328
        ),
    )(queries, keys, values, feat_weight, norm_gain.reshape(1, -1), counts, offsets)

def per_device(n, queries, keys, values, feat_weight, norm_gain, counts, offsets):
    rows = queries.shape[0]
    heads, width, feat = feat_weight.shape
    if n != heads or n % 4 or n > rows or rows % (8 * TILE):
        return grouped(n, queries, keys, values, feat_weight, norm_gain, counts, offsets)
    lanes = 2 * width
    tiles = rows // TILE
    tokens = n * TILE
    total = n * rows
    cut = tiles * 3 // 4
    parts = ((0, cut), (cut, tiles))
    returns = ((0, 4), (4, tiles))
    return pl.pallas_call(
        functools.partial(kernel, n, parts, returns),
        out_shape=pltpu.VMEM(queries.shape, BF16),
        in_specs=[pl.BlockSpec(memory_space=pltpu.HBM)] * 7,
        out_specs=pl.BlockSpec(memory_space=pltpu.VMEM),
        scratch_shapes=[
            pltpu.VMEM(queries.shape, BF16),
            pltpu.VMEM(keys.shape, BF16),
            pltpu.VMEM(values.shape, BF16),
            pltpu.VMEM((width, feat), BF16),
            pltpu.VMEM(norm_gain.shape, BF16),
            pltpu.VMEM(counts.shape, jnp.int32),
            pltpu.VMEM(offsets.shape, jnp.int32),
            pltpu.SemaphoreType.DMA((7,)),
            pltpu.VMEM((n, rows + rows // 2, lanes), BF16),
            pltpu.VMEM((n, rows + rows // 2, lanes), BF16),
            pltpu.VMEM((total, feat), BF16),
            pltpu.VMEM((feat, total), BF16),
            pltpu.VMEM((total, width), BF16),
            pltpu.VMEM((rows, max(n, rows)), F32),
            pltpu.VMEM((tiles, 8, tokens), F32),
            pltpu.VMEM((tiles, n, TILE, 128), F32),
            pltpu.VMEM((tiles, feat, lanes), BF16),
            pltpu.VMEM((lanes, feat), BF16),
            pltpu.VMEM((feat, lanes), BF16),
            pltpu.VMEM((n, rows // 2, lanes), BF16),
            pltpu.VMEM((n, rows // 2, lanes), BF16),
            pltpu.SemaphoreType.DMA((n, len(parts))),
            pltpu.SemaphoreType.DMA((n, len(parts))),
            pltpu.SemaphoreType.DMA((n, len(returns))),
            pltpu.SemaphoreType.DMA((n, len(returns))),
            pltpu.SemaphoreType.REGULAR((2,)),
        ],
        compiler_params=pltpu.CompilerParams(
            collective_id=0, has_side_effects=True, vmem_limit_bytes=60000000
        ),
    )(queries, keys, values, feat_weight, norm_gain, counts, offsets)


def solution(mesh):
    in_specs = (
        P(("dp", "seq"), None),
        P(("dp", "seq"), None),
        P(("dp", "seq"), None),
        P(),
        P(),
        P("dp", None),
        P("dp", None),
    )
    return jax.shard_map(
        functools.partial(per_device, mesh.shape["seq"]),
        mesh=mesh,
        in_specs=in_specs,
        out_specs=P(("dp", "seq"), None),
        check_vma=False,
    )
```

```python
import functools

import jax
import jax.numpy as jnp
from jax import lax
from jax.experimental import pallas as pl
from jax.experimental.pallas import tpu as pltpu
from jax.sharding import PartitionSpec as P

MESH = pl.DeviceIdType.MESH
F32 = jnp.float32
BF16 = jnp.bfloat16
GROUPS = 4
TILE = 16


def block_bounds(n, rows, i):
    least = rows // n // 2
    most = 3 * (rows // n) // 2
    first = min(d for d in range(n) if min(most * (d + 1), rows - least * (n - d - 1)) > i)
    last = max(d for d in range(n) if max(least * d, rows - most * (n - d)) <= i)
    return first, last


def kernel(
    n,
    parts,
    returns,
    q_ref,
    k_ref,
    v_ref,
    w_ref,
    gain_ref,
    counts_ref,
    offsets_ref,
    out_ref,
    q_buf,
    k_buf,
    v_buf,
    w_buf,
    gain_buf,
    counts_buf,
    offsets_buf,
    load_sem,
    send,
    recv,
    phi_q,
    phi_kt,
    val,
    post,
    slot_row,
    slot_col,
    acc,
    state,
    wq,
    wkt,
    out_send,
    out_recv,
    send_sem,
    recv_sem,
    back_send_sem,
    back_recv_sem,
    stage_sem,
):
    rows = q_ref.shape[0]
    width = q_ref.shape[1] // n
    tiles = rows // TILE
    tokens = n * TILE
    me = lax.axis_index("seq")

    bounds = [
        (block_bounds(n, rows, TILE * a)[0], block_bounds(n, rows, TILE * a + TILE - 1)[1])
        for a in range(tiles)
    ]
    full = [sum(1 for b in range(tiles) if bounds[b][1] < bounds[a][0]) for a in range(tiles)]
    ends = [sum(1 for b in range(tiles) if bounds[b][0] <= bounds[a][1]) for a in range(tiles)]

    half = n // 2
    own = me // half * half

    def near(dev):
        return lax.rem(dev + n - own, n)

    def near_for(peer):
        return lax.rem(me + n - peer // half * half, n)

    loads = [
        pltpu.make_async_copy(src, dst, load_sem.at[i])
        for i, (src, dst) in enumerate(
            (
                (q_ref, q_buf),
                (k_ref, k_buf),
                (v_ref, v_buf),
                (counts_ref, counts_buf),
                (offsets_ref, offsets_buf),
                (w_ref.at[me], w_buf),
                (gain_ref, gain_buf),
            )
        )
    ]
    for load in loads:
        load.start()

    def hops(peer):
        across = jnp.abs(peer // 4 - me // 4)
        return across + jnp.abs(peer // 2 % 2 - me // 2 % 2)

    def each(order, do):
        def body(step, carry):
            do(order(step))
            return carry

        lax.fori_loop(1, n, body, 0)

    def swap(step):
        return me ^ step

    def ahead(step):
        return lax.rem(me + step, n)

    def behind(step):
        return lax.rem(me + n - step, n)

    def tell(sem, reach):
        def one(peer):
            @pl.when(hops(peer) <= reach)
            def _():
                pl.semaphore_signal(sem, inc=1, device_id={"seq": peer}, device_id_type=MESH)

        each(swap, one)

    def within(reach):
        return sum(jnp.where(hops(me ^ step) <= reach, 1, 0) for step in range(1, n))

    stages = [1, 1, max(n // 4 - 2, 1)]
    barrier = pltpu.get_barrier_semaphore()
    tell(barrier, stages[0])

    for load in loads[:3]:
        load.wait()

    starts = []
    at = 0
    for first, last in parts:
        starts.append((at, at + (last - first) * TILE, at + (last - first) * (TILE + TILE // 2)))
        at = starts[-1][2]

    for pair in range(n // 2):
        lanes = slice(2 * width * pair, 2 * width * (pair + 1))
        q = q_buf[:, lanes]
        k = k_buf[:, lanes]
        v = v_buf[:, lanes]
        for (first, last), (base, mid, end) in zip(parts, starts):
            here = slice(first * TILE, last * TILE)
            send[2 * pair, base:mid, :] = jnp.concatenate([q[here, :width], k[here, :width]], axis=1)
            send[2 * pair + 1, base:mid, :] = jnp.concatenate([q[here, width:], k[here, width:]], axis=1)
            for a in range(first, last, 2):
                to = slice(mid + (a - first) * TILE // 2, mid + (a - first + 2) * TILE // 2)
                even = v[a * TILE : (a + 1) * TILE]
                odd = v[(a + 1) * TILE : (a + 2) * TILE]
                send[2 * pair, to, :] = jnp.concatenate([even[:, :width], odd[:, :width]], axis=1)
                send[2 * pair + 1, to, :] = jnp.concatenate([even[:, width:], odd[:, width:]], axis=1)

    def forward(peer, g):
        piece = slice(starts[g][0], starts[g][2])
        return pltpu.make_async_remote_copy(
            src_ref=send.at[peer, piece],
            dst_ref=recv.at[near_for(peer), piece],
            send_sem=send_sem.at[peer, g],
            recv_sem=recv_sem.at[me, g],
            device_id={"seq": peer},
            device_id_type=MESH,
        )

    def arrive(src, g):
        piece = slice(starts[g][0], starts[g][2])
        pltpu.make_async_remote_copy(
            src_ref=send.at[src, piece],
            dst_ref=recv.at[near(src), piece],
            send_sem=send_sem.at[src, g],
            recv_sem=recv_sem.at[src, g],
            device_id={"seq": src},
            device_id_type=MESH,
        ).wait_recv()

    def send_between(low, high):
        def one(peer):
            @pl.when((hops(peer) > low) & (hops(peer) <= high))
            def _():
                forward(peer, 0).start()

        each(swap, one)

    pl.semaphore_wait(barrier, within(stages[0]))
    tell(stage_sem.at[0], stages[1])
    send_between(-1, stages[0])
    recv[near(me)] = send[me]

    for load in loads[3:]:
        load.wait()
    lane = lax.broadcasted_iota(jnp.int32, (n, rows), 1)
    start = jnp.zeros((n, 1), jnp.int32)
    position = lane
    for d in range(n):
        count = counts_buf[:, d : d + 1]
        inside = (lane >= start) & (lane < start + count)
        position = position + jnp.where(inside, d * rows + offsets_buf[:, d : d + 1] - start, 0)
        start = start + count
    position = position.astype(F32)

    pl.semaphore_wait(stage_sem.at[0], within(stages[1]))
    tell(stage_sem.at[1], stages[2])
    send_between(stages[0], stages[0] + stages[1])

    if n < rows:
        position = jnp.concatenate([position, jnp.zeros((rows - n, rows), F32)], axis=0)
    post[...] = position.T

    pl.semaphore_wait(stage_sem.at[1], within(stages[2]))
    send_between(stages[0] + stages[1], n)
    for g in range(1, len(parts)):
        for step in range(1, half):
            forward(own + lax.rem(me + step, half), g).start()

    for j in range(n):
        column = jnp.broadcast_to(post[:, j : j + 1], (rows, 128))
        slot_col[:, near(j)] = column.reshape(tiles, TILE, 128)
    for a in range(tiles):
        slot_row[a] = slot_col[a].reshape(tokens, 128).T[0:8, :]

    w = w_buf[...]
    blank = jnp.zeros_like(w)
    wq[...] = jnp.concatenate([w, blank], axis=0)
    wkt[...] = jnp.concatenate([blank, w], axis=0).astype(F32).T.astype(BF16)
    gains = gain_buf[...].astype(F32).reshape(1, n * width)
    gain = jnp.zeros((1, width), F32)
    for h in range(n):
        gain = gain + jnp.where(me == h, gains[:, h * width : (h + 1) * width], 0.0)

    def feature(z):
        return jnp.where(z > 0.0, z + 1.0, jnp.exp(jnp.minimum(z, 0.0))).astype(BF16)

    share = tokens // 2

    def take(a, part):
        g = next(i for i, (first, last) in enumerate(parts) if first <= a < last)
        first = parts[g][0]
        base, mid, _ = starts[g]
        here = slice(base + (a - first) * TILE, base + (a - first + 1) * TILE)
        group = slice(part * half, (part + 1) * half)
        slots = slice(a * tokens + part * share, a * tokens + (part + 1) * share)
        x = recv[group, here, :].reshape(share, 2 * width)
        phi_q[slots, :] = feature(jnp.dot(x, wq[...], preferred_element_type=F32))
        keys = lax.dot_general(wkt[...], x, (((1,), (1,)), ((), ())), preferred_element_type=F32)
        phi_kt[:, slots] = feature(keys)
        there = mid + (a - first) // 2 * TILE
        v = recv[group, there : there + TILE, :].reshape(share, 2 * width)
        val[slots, :] = v[:, width:] if a % 2 else v[:, :width]

    def tile(a, count, b0, b1):
        size = count * tokens
        span = (b1 - b0) * tokens
        scores = jnp.dot(
            phi_q[a * tokens : a * tokens + size, :],
            phi_kt[:, b0 * tokens : b1 * tokens],
            preferred_element_type=F32,
        )
        later = slot_col[a : a + count].reshape(size // 8, 8, 128)
        later = jnp.concatenate([later] * (span // 128), axis=2)
        earlier = jnp.concatenate([slot_row[b] for b in range(b0, b1)], axis=1)
        keep = earlier[None] <= later
        scores = jnp.where(keep, scores.reshape(size // 8, 8, span), 0.0).reshape(size, span)
        high = scores.astype(BF16)
        low = (scores - high.astype(F32)).astype(BF16)
        both = jnp.dot(
            jnp.concatenate([high, low], axis=0),
            val[b0 * tokens : b1 * tokens, :],
            preferred_element_type=F32,
        )
        return both[:size] + both[size:]

    marks = sorted(set(f for f in full if f))

    sums = []

    def add_state():
        b0 = marks[len(sums) - 1] if sums else 0
        b1 = marks[len(sums)]
        total = jnp.dot(
            phi_kt[:, b0 * tokens : b1 * tokens],
            val[b0 * tokens : b1 * tokens, :],
            preferred_element_type=F32,
        )
        if sums:
            total = sums[-1] + total
        high = total.astype(BF16)
        low = (total - high.astype(F32)).astype(BF16)
        state[len(sums)] = jnp.concatenate([high, low], axis=1)
        sums.append(total)

    def from_state(a):
        while len(sums) <= marks.index(full[a]):
            add_state()
        both = jnp.dot(
            phi_q[a * tokens : (a + 1) * tokens, :], state[marks.index(full[a])], preferred_element_type=F32
        )
        return both[:, :width] + both[:, width:]

    def sweep(a, count, b0, b1, step):
        total = None
        for b in range(b0, b1, step):
            piece = tile(a, count, b, min(b + step, b1))
            total = piece if total is None else total + piece
        return total

    def normalise(attended):
        centre = jnp.mean(attended, axis=1, keepdims=True)
        centred = attended - centre
        spread = jnp.mean(centred * centred, axis=1, keepdims=True)
        return (centred * lax.rsqrt(spread + 1e-05) * gain).astype(BF16)

    def pack(a, even, odd):
        y = jnp.concatenate([even, odd], axis=1).reshape(n, TILE, 2 * width)
        out_send[:, a * TILE // 2 : a * TILE // 2 + TILE, :] = y

    def piece_of(g):
        return slice(returns[g][0] * TILE // 2, returns[g][1] * TILE // 2)

    def back(loader, g):
        return pltpu.make_async_remote_copy(
            src_ref=out_send.at[near(loader), piece_of(g)],
            dst_ref=out_recv.at[me, piece_of(g)],
            send_sem=back_send_sem.at[loader, g],
            recv_sem=back_recv_sem.at[me, g],
            device_id={"seq": loader},
            device_id_type=MESH,
        )

    def collect(src, g):
        pltpu.make_async_remote_copy(
            src_ref=out_send.at[src, piece_of(g)],
            dst_ref=out_recv.at[src, piece_of(g)],
            send_sem=back_send_sem.at[src, g],
            recv_sem=back_recv_sem.at[src, g],
            device_id={"seq": src},
            device_id_type=MESH,
        ).wait_recv()

    for g, (first, last) in enumerate(parts):
        for step in range(1, half):
            arrive(own + lax.rem(me + step, half), g)
        for a in range(first, last):
            take(a, 0)

    sent = 0
    done = {}
    for g, (first, last) in enumerate(parts):
        def cross(i, carry):
            peer = lax.rem(own + half + lax.rem(me + i, half), n)
            arrive(peer, g)
            return carry

        lax.fori_loop(0, half, cross, 0)
        if g + 1 < len(parts):
            def onward(i, carry):
                forward(lax.rem(own + half + lax.rem(me + i, half), n), g + 1).start()
                return carry

            lax.fori_loop(0, half, onward, 0)
        for b in range(first, last):
            take(b, 1)
        for a in range(last):
            if a < first and ends[a] <= first:
                continue
            total = sweep(a, 1, max(full[a], first if a < first else 0), min(ends[a], last), 3)
            if a < first:
                total = total + acc[a]
            elif full[a]:
                total = total + from_state(a)
            if ends[a] > last:
                acc[a] = total
                continue
            done[a] = normalise(total)
            if a % 2:
                pack(a - 1, done.pop(a - 1), done.pop(a))
            while sent < len(returns) and returns[sent][1] <= a + 1 and a % 2:
                each(ahead, lambda loader: back(loader, sent).start())
                sent += 1
        while len(sums) < len(marks) and marks[len(sums)] <= last:
            add_state()

    out_recv[me] = out_send[near(me)]
    for g, (first, last) in enumerate(returns):
        each(behind, lambda src: collect(src, g))
        for a in range(first, last, 2):
            here = slice(a * TILE // 2, a * TILE // 2 + TILE)
            for pair in range(n // 2):
                lanes = slice(2 * width * pair, 2 * width * (pair + 1))
                x = out_recv[2 * pair, here, :]
                y = out_recv[2 * pair + 1, here, :]
                out_ref[a * TILE : (a + 1) * TILE, lanes] = jnp.concatenate(
                    [x[:, :width], y[:, :width]], axis=1
                )
                out_ref[(a + 1) * TILE : (a + 2) * TILE, lanes] = jnp.concatenate(
                    [x[:, width:], y[:, width:]], axis=1
                )

    def drain(peer):
        for g in range(len(parts)):
            forward(peer, g).wait_send()
        for g in range(len(returns)):
            back(peer, g).wait_send()

    each(ahead, drain)


def grouped_kernel(
    n,
    heads,
    q_ref,
    k_ref,
    v_ref,
    w_ref,
    gain_ref,
    counts_ref,
    offsets_ref,
    out_ref,
    q_buf,
    k_buf,
    v_buf,
    w_buf,
    gain_buf,
    counts_buf,
    offsets_buf,
    load_sem,
    send,
    recv,
    phi_q,
    phi_kt,
    val,
    posr,
    post,
    posc,
    slot_row,
    slot_col,
    acc,
    wq,
    wkt,
    out_send,
    out_recv,
    send_sem,
    recv_sem,
    back_send_sem,
    back_recv_sem,
):
    rows = q_ref.shape[0]
    half = rows // 2
    width = q_ref.shape[1] // heads
    feat = w_ref.shape[2]
    group = n // heads
    part_rows = rows // group
    part_half = part_rows // 2
    total = n * rows
    queries = n * part_rows
    me = lax.axis_index("seq")
    head = me // group
    part = me % group

    half_ring = n // 2
    own = me // half_ring * half_ring
    other = lax.rem(own + half_ring, n)

    def target(step):
        return jnp.where(step < half_ring, own, other) + lax.rem(me + step, half_ring)

    def source(step):
        return jnp.where(step < half_ring, own, other) + lax.rem(me + n - step, half_ring)

    loads = [
        pltpu.make_async_copy(src, dst, load_sem.at[i])
        for i, (src, dst) in enumerate(
            (
                (q_ref, q_buf),
                (k_ref, k_buf),
                (v_ref, v_buf),
                (counts_ref, counts_buf),
                (offsets_ref, offsets_buf),
                (w_ref.at[head], w_buf),
                (gain_ref, gain_buf),
            )
        )
    ]
    for load in loads:
        load.start()

    barrier = pltpu.get_barrier_semaphore()

    def greet(step, carry):
        peer = lax.rem(me + step, n)
        pl.semaphore_signal(barrier, inc=1, device_id={"seq": peer}, device_id_type=MESH)
        return carry

    lax.fori_loop(1, n, greet, 0)

    for load in loads[:3]:
        load.wait()

    for pair in range(heads // 2):
        lanes = slice(2 * width * pair, 2 * width * (pair + 1))
        q = q_buf[:, lanes]
        k = k_buf[:, lanes]
        v = v_buf[:, lanes]
        send[2 * pair, 0:rows, :] = jnp.concatenate([q[:, :width], k[:, :width]], axis=1)
        send[2 * pair + 1, 0:rows, :] = jnp.concatenate([q[:, width:], k[:, width:]], axis=1)
        send[2 * pair, rows:, :] = jnp.concatenate([v[:half, :width], v[half:, :width]], axis=1)
        send[2 * pair + 1, rows:, :] = jnp.concatenate([v[:half, width:], v[half:, width:]], axis=1)

    pl.semaphore_wait(barrier, n - 1)

    def forward(peer):
        return pltpu.make_async_remote_copy(
            src_ref=send.at[peer // group],
            dst_ref=recv.at[me],
            send_sem=send_sem.at[peer],
            recv_sem=recv_sem.at[me],
            device_id={"seq": peer},
            device_id_type=MESH,
        )

    def send_one(step, carry):
        forward(target(step)).start()
        return carry

    lax.fori_loop(1, n, send_one, 0)
    recv[me] = send[head]

    for load in loads[3:]:
        load.wait()

    lane = lax.broadcasted_iota(jnp.int32, (n, rows), 1)
    start = jnp.zeros((n, 1), jnp.int32)
    position = lane
    for d in range(n):
        count = counts_buf[:, d : d + 1]
        inside = (lane >= start) & (lane < start + count)
        position = position + jnp.where(inside, d * rows + offsets_buf[:, d : d + 1] - start, 0)
        start = start + count
    position = position.astype(F32)
    posr[...] = position
    if n < rows:
        position = jnp.concatenate([position, jnp.zeros((rows - n, rows), F32)], axis=0)
    post[...] = position.T
    mine = post[pl.ds(pl.multiple_of(part * part_rows, part_rows), part_rows), :]
    for j in range(n):
        posc[j * part_rows : (j + 1) * part_rows, :] = jnp.broadcast_to(
            mine[:, j : j + 1], (part_rows, 128)
        )

    w = w_buf[...]
    blank = jnp.zeros_like(w)
    wq[...] = jnp.concatenate([w, blank], axis=0)
    wkt[...] = jnp.concatenate([blank, w], axis=0).astype(F32).T.astype(BF16)
    gain = jnp.zeros((1, width), F32)
    for h in range(heads):
        gain = gain + jnp.where(head == h, gain_buf[:, h * width : (h + 1) * width].astype(F32), 0.0)

    def feature(z):
        return jnp.where(z > 0.0, z + 1.0, jnp.exp(jnp.minimum(z, 0.0))).astype(BF16)

    def take_block(step):
        src = source(step)
        x = recv[src, 0:rows, :]
        keys = lax.dot_general(wkt[...], x, (((1,), (1,)), ((), ())), preferred_element_type=F32)
        phi_kt[:, step * rows : (step + 1) * rows] = feature(keys)
        mine_of = pl.multiple_of(part * part_rows, part_rows)
        proj = jnp.dot(
            recv[src, pl.ds(mine_of, part_rows), :], wq[...], preferred_element_type=F32
        )
        slots = slice(step * part_rows, (step + 1) * part_rows)
        phi_q[slots, :] = feature(proj)
        block = recv[src, rows:, :]
        val[step * rows : step * rows + half, :] = block[:, :width]
        val[step * rows + half : (step + 1) * rows, :] = block[:, width:]
        slot_row[step : step + 1, :] = posr[pl.ds(src, 1), :]
        slot_col[slots, :] = posc[
            pl.ds(pl.multiple_of(src * part_rows, part_rows), part_rows), :
        ]

    def arrive(step):
        src = source(step)
        pltpu.make_async_remote_copy(
            src_ref=send.at[0],
            dst_ref=recv.at[src],
            send_sem=send_sem.at[src],
            recv_sem=recv_sem.at[src],
            device_id={"seq": src},
            device_id_type=MESH,
        ).wait_recv()

    groups = min(GROUPS, n)
    per = n // groups
    tile_r = per * part_rows
    tile_s = per * rows

    def tile(rb, sb):
        r0 = pl.multiple_of(rb * tile_r, tile_r)
        s0 = pl.multiple_of(sb * tile_s, tile_s)
        scores = jnp.dot(
            phi_q[pl.ds(r0, tile_r), :], phi_kt[:, pl.ds(s0, tile_s)], preferred_element_type=F32
        )
        later = jnp.concatenate([slot_col[pl.ds(r0, tile_r), :]] * per, axis=1)
        earlier = jnp.concatenate([slot_row[pl.ds(sb * per + i, 1), :] for i in range(per)], axis=1)
        scores = jnp.where(earlier <= later, scores, 0.0)
        high = scores.astype(BF16)
        low = (scores - high.astype(F32)).astype(BF16)
        vals = val[pl.ds(s0, tile_s), :]
        return jnp.dot(high, vals, preferred_element_type=F32) + jnp.dot(
            low, vals, preferred_element_type=F32
        )

    def back(step):
        loader = source(step)
        return pltpu.make_async_remote_copy(
            src_ref=out_send.at[step],
            dst_ref=out_recv.at[me],
            send_sem=back_send_sem.at[loader],
            recv_sem=back_recv_sem.at[me],
            device_id={"seq": loader},
            device_id_type=MESH,
        )

    def finish(rb, attended):
        centre = jnp.mean(attended, axis=1, keepdims=True)
        centred = attended - centre
        spread = jnp.mean(centred * centred, axis=1, keepdims=True)
        normed = (centred * lax.rsqrt(spread + 1e-05) * gain).astype(BF16)
        for i in range(per):
            y = normed[i * part_rows : (i + 1) * part_rows]
            out_send[rb * per + i] = jnp.concatenate([y[:part_half], y[part_half:]], axis=1)
        for i in range(per):
            if rb * per + i > 0:
                back(rb * per + i).start()

    def rows_of(rb):
        return pl.ds(pl.multiple_of(rb * tile_r, tile_r), tile_r)

    for gi in range(groups):
        for step in range(gi * per, (gi + 1) * per):
            if step > 0:
                arrive(step)
            take_block(step)
        last = gi == groups - 1
        fresh = tile(gi, gi)
        if not last:

            def both(i, fresh):
                acc[rows_of(i), :] = acc[rows_of(i), :] + tile(i, gi)
                return fresh + tile(gi, i)

            acc[rows_of(gi), :] = lax.fori_loop(0, gi, both, fresh)
        else:
            finish(gi, lax.fori_loop(0, gi, lambda i, fresh: fresh + tile(gi, i), fresh))
            for i in reversed(range(gi)):
                finish(i, acc[rows_of(i), :] + tile(i, gi))
    out_recv[me] = out_send[0]

    def collect(step, carry):
        src = source(step)
        pltpu.make_async_remote_copy(
            src_ref=out_send.at[step],
            dst_ref=out_recv.at[src],
            send_sem=back_send_sem.at[src],
            recv_sem=back_recv_sem.at[src],
            device_id={"seq": src},
            device_id_type=MESH,
        ).wait_recv()
        return carry

    lax.fori_loop(1, n, collect, 0)

    for piece in range(group):
        first = slice(piece * part_rows, piece * part_rows + part_half)
        second = slice(piece * part_rows + part_half, (piece + 1) * part_rows)
        for pair in range(heads // 2):
            lanes = slice(2 * width * pair, 2 * width * (pair + 1))
            a = out_recv[2 * pair * group + piece]
            b = out_recv[(2 * pair + 1) * group + piece]
            out_ref[first, lanes] = jnp.concatenate([a[:, :width], b[:, :width]], axis=1)
            out_ref[second, lanes] = jnp.concatenate([a[:, width:], b[:, width:]], axis=1)

    def drain(step, carry):
        peer = target(step)
        forward(peer).wait_send()
        back(step).wait_send()
        return carry

    lax.fori_loop(1, n, drain, 0)


def grouped(n, queries, keys, values, feat_weight, norm_gain, counts, offsets):
    rows = queries.shape[0]
    heads, width, feat = feat_weight.shape
    group = n // heads
    part_rows = rows // group
    total = n * rows
    lanes = 2 * width
    return pl.pallas_call(
        functools.partial(grouped_kernel, n, heads),
        out_shape=jax.ShapeDtypeStruct(queries.shape, BF16),
        in_specs=[pl.BlockSpec(memory_space=pltpu.HBM)] * 7,
        out_specs=pl.BlockSpec(memory_space=pltpu.VMEM),
        scratch_shapes=[
            pltpu.VMEM(queries.shape, BF16),
            pltpu.VMEM(keys.shape, BF16),
            pltpu.VMEM(values.shape, BF16),
            pltpu.VMEM((width, feat), BF16),
            pltpu.VMEM((1, norm_gain.shape[0]), BF16),
            pltpu.VMEM(counts.shape, jnp.int32),
            pltpu.VMEM(offsets.shape, jnp.int32),
            pltpu.SemaphoreType.DMA((7,)),
            pltpu.VMEM((heads, rows + rows // 2, lanes), BF16),
            pltpu.VMEM((n, rows + rows // 2, lanes), BF16),
            pltpu.VMEM((n * part_rows, feat), BF16),
            pltpu.VMEM((feat, total), BF16),
            pltpu.VMEM((total, width), BF16),
            pltpu.VMEM((n, rows), F32),
            pltpu.VMEM((rows, max(n, rows)), F32),
            pltpu.VMEM((n * part_rows, 128), F32),
            pltpu.VMEM((n, rows), F32),
            pltpu.VMEM((n * part_rows, 128), F32),
            pltpu.VMEM((n * part_rows, width), F32),
            pltpu.VMEM((lanes, feat), BF16),
            pltpu.VMEM((feat, lanes), BF16),
            pltpu.VMEM((n, part_rows // 2, lanes), BF16),
            pltpu.VMEM((n, part_rows // 2, lanes), BF16),
            pltpu.SemaphoreType.DMA((n,)),
            pltpu.SemaphoreType.DMA((n,)),
            pltpu.SemaphoreType.DMA((n,)),
            pltpu.SemaphoreType.DMA((n,)),
        ],
        compiler_params=pltpu.CompilerParams(
            collective_id=0, has_side_effects=True, vmem_limit_bytes=67043328
        ),
    )(queries, keys, values, feat_weight, norm_gain.reshape(1, -1), counts, offsets)

def per_device(n, queries, keys, values, feat_weight, norm_gain, counts, offsets):
    rows = queries.shape[0]
    heads, width, feat = feat_weight.shape
    if n != heads or n % 4 or n > rows or rows % (8 * TILE):
        return grouped(n, queries, keys, values, feat_weight, norm_gain, counts, offsets)
    lanes = 2 * width
    tiles = rows // TILE
    tokens = n * TILE
    total = n * rows
    cut = tiles * 3 // 4
    parts = ((0, cut), (cut, tiles))
    returns = ((0, 2), (2, tiles))
    return pl.pallas_call(
        functools.partial(kernel, n, parts, returns),
        out_shape=pltpu.VMEM(queries.shape, BF16),
        in_specs=[pl.BlockSpec(memory_space=pltpu.HBM)] * 7,
        out_specs=pl.BlockSpec(memory_space=pltpu.VMEM),
        scratch_shapes=[
            pltpu.VMEM(queries.shape, BF16),
            pltpu.VMEM(keys.shape, BF16),
            pltpu.VMEM(values.shape, BF16),
            pltpu.VMEM((width, feat), BF16),
            pltpu.VMEM(norm_gain.shape, BF16),
            pltpu.VMEM(counts.shape, jnp.int32),
            pltpu.VMEM(offsets.shape, jnp.int32),
            pltpu.SemaphoreType.DMA((7,)),
            pltpu.VMEM((n, rows + rows // 2, lanes), BF16),
            pltpu.VMEM((n, rows + rows // 2, lanes), BF16),
            pltpu.VMEM((total, feat), BF16),
            pltpu.VMEM((feat, total), BF16),
            pltpu.VMEM((total, width), BF16),
            pltpu.VMEM((rows, max(n, rows)), F32),
            pltpu.VMEM((tiles, 8, tokens), F32),
            pltpu.VMEM((tiles, n, TILE, 128), F32),
            pltpu.VMEM((tiles, tokens, width), F32),
            pltpu.VMEM((tiles, feat, lanes), BF16),
            pltpu.VMEM((lanes, feat), BF16),
            pltpu.VMEM((feat, lanes), BF16),
            pltpu.VMEM((n, rows // 2, lanes), BF16),
            pltpu.VMEM((n, rows // 2, lanes), BF16),
            pltpu.SemaphoreType.DMA((n, len(parts))),
            pltpu.SemaphoreType.DMA((n, len(parts))),
            pltpu.SemaphoreType.DMA((n, len(returns))),
            pltpu.SemaphoreType.DMA((n, len(returns))),
            pltpu.SemaphoreType.REGULAR((2,)),
        ],
        compiler_params=pltpu.CompilerParams(
            collective_id=0, has_side_effects=True, vmem_limit_bytes=60000000
        ),
    )(queries, keys, values, feat_weight, norm_gain, counts, offsets)


def solution(mesh):
    in_specs = (
        P(("dp", "seq"), None),
        P(("dp", "seq"), None),
        P(("dp", "seq"), None),
        P(),
        P(),
        P("dp", None),
        P("dp", None),
    )
    return jax.shard_map(
        functools.partial(per_device, mesh.shape["seq"]),
        mesh=mesh,
        in_specs=in_specs,
        out_specs=P(("dp", "seq"), None),
        check_vma=False,
    )
```

```python
import functools

import jax
import jax.numpy as jnp
from jax import lax
from jax.experimental import pallas as pl
from jax.experimental.pallas import tpu as pltpu
from jax.sharding import PartitionSpec as P

MESH = pl.DeviceIdType.MESH
F32 = jnp.float32
BF16 = jnp.bfloat16
GROUPS = 4
TILE = 16


def block_bounds(n, rows, i):
    least = rows // n // 2
    most = 3 * (rows // n) // 2
    first = min(d for d in range(n) if min(most * (d + 1), rows - least * (n - d - 1)) > i)
    last = max(d for d in range(n) if max(least * d, rows - most * (n - d)) <= i)
    return first, last


def kernel(
    n,
    parts,
    returns,
    q_ref,
    k_ref,
    v_ref,
    w_ref,
    gain_ref,
    counts_ref,
    offsets_ref,
    out_ref,
    q_buf,
    k_buf,
    v_buf,
    w_buf,
    gain_buf,
    counts_buf,
    offsets_buf,
    load_sem,
    send,
    recv,
    phi_q,
    phi_kt,
    val,
    post,
    slot_row,
    slot_col,
    acc,
    state,
    wq,
    wkt,
    out_send,
    out_recv,
    send_sem,
    recv_sem,
    back_send_sem,
    back_recv_sem,
    stage_sem,
):
    rows = q_ref.shape[0]
    width = q_ref.shape[1] // n
    tiles = rows // TILE
    tokens = n * TILE
    me = lax.axis_index("seq")

    bounds = [
        (block_bounds(n, rows, TILE * a)[0], block_bounds(n, rows, TILE * a + TILE - 1)[1])
        for a in range(tiles)
    ]
    full = [sum(1 for b in range(tiles) if bounds[b][1] < bounds[a][0]) for a in range(tiles)]
    ends = [sum(1 for b in range(tiles) if bounds[b][0] <= bounds[a][1]) for a in range(tiles)]

    half = n // 2
    own = me // half * half

    def near(dev):
        return lax.rem(dev + n - own, n)

    def near_for(peer):
        return lax.rem(me + n - peer // half * half, n)

    loads = [
        pltpu.make_async_copy(src, dst, load_sem.at[i])
        for i, (src, dst) in enumerate(
            (
                (q_ref, q_buf),
                (k_ref, k_buf),
                (v_ref, v_buf),
                (counts_ref, counts_buf),
                (offsets_ref, offsets_buf),
                (w_ref.at[me], w_buf),
                (gain_ref, gain_buf),
            )
        )
    ]
    for load in loads:
        load.start()

    def hops(peer):
        across = jnp.abs(peer // 4 - me // 4)
        return across + jnp.abs(peer // 2 % 2 - me // 2 % 2)

    def each(order, do):
        def body(step, carry):
            do(order(step))
            return carry

        lax.fori_loop(1, n, body, 0)

    def every(order, do):
        for step in range(1, n):
            do(order(step))

    def swap(step):
        return me ^ step

    def ahead(step):
        return lax.rem(me + step, n)

    def behind(step):
        return lax.rem(me + n - step, n)

    def tell(sem, reach):
        def one(peer):
            @pl.when(hops(peer) <= reach)
            def _():
                pl.semaphore_signal(sem, inc=1, device_id={"seq": peer}, device_id_type=MESH)

        each(swap, one)

    def within(reach):
        return sum(jnp.where(hops(me ^ step) <= reach, 1, 0) for step in range(1, n))

    stages = [1, 1, max(n // 4 - 2, 1)]
    barrier = pltpu.get_barrier_semaphore()
    tell(barrier, stages[0])

    for load in loads[:3]:
        load.wait()

    starts = []
    at = 0
    for first, last in parts:
        starts.append((at, at + (last - first) * TILE, at + (last - first) * (TILE + TILE // 2)))
        at = starts[-1][2]

    for pair in range(n // 2):
        lanes = slice(2 * width * pair, 2 * width * (pair + 1))
        q = q_buf[:, lanes]
        k = k_buf[:, lanes]
        v = v_buf[:, lanes]
        for (first, last), (base, mid, end) in zip(parts, starts):
            here = slice(first * TILE, last * TILE)
            send[2 * pair, base:mid, :] = jnp.concatenate([q[here, :width], k[here, :width]], axis=1)
            send[2 * pair + 1, base:mid, :] = jnp.concatenate([q[here, width:], k[here, width:]], axis=1)
            for a in range(first, last, 2):
                to = slice(mid + (a - first) * TILE // 2, mid + (a - first + 2) * TILE // 2)
                even = v[a * TILE : (a + 1) * TILE]
                odd = v[(a + 1) * TILE : (a + 2) * TILE]
                send[2 * pair, to, :] = jnp.concatenate([even[:, :width], odd[:, :width]], axis=1)
                send[2 * pair + 1, to, :] = jnp.concatenate([even[:, width:], odd[:, width:]], axis=1)

    def forward(peer, g):
        piece = slice(starts[g][0], starts[g][2])
        return pltpu.make_async_remote_copy(
            src_ref=send.at[peer, piece],
            dst_ref=recv.at[near_for(peer), piece],
            send_sem=send_sem.at[peer, g],
            recv_sem=recv_sem.at[me, g],
            device_id={"seq": peer},
            device_id_type=MESH,
        )

    def arrive(src, g):
        piece = slice(starts[g][0], starts[g][2])
        pltpu.make_async_remote_copy(
            src_ref=send.at[src, piece],
            dst_ref=recv.at[near(src), piece],
            send_sem=send_sem.at[src, g],
            recv_sem=recv_sem.at[src, g],
            device_id={"seq": src},
            device_id_type=MESH,
        ).wait_recv()

    def send_between(low, high):
        def one(peer):
            @pl.when((hops(peer) > low) & (hops(peer) <= high))
            def _():
                forward(peer, 0).start()

        each(swap, one)

    pl.semaphore_wait(barrier, within(stages[0]))
    tell(stage_sem.at[0], stages[1])
    send_between(-1, stages[0])
    recv[near(me)] = send[me]

    for load in loads[3:]:
        load.wait()
    lane = lax.broadcasted_iota(jnp.int32, (n, rows), 1)
    start = jnp.zeros((n, 1), jnp.int32)
    position = lane
    for d in range(n):
        count = counts_buf[:, d : d + 1]
        inside = (lane >= start) & (lane < start + count)
        position = position + jnp.where(inside, d * rows + offsets_buf[:, d : d + 1] - start, 0)
        start = start + count
    position = position.astype(F32)

    pl.semaphore_wait(stage_sem.at[0], within(stages[1]))
    tell(stage_sem.at[1], stages[2])
    send_between(stages[0], stages[0] + stages[1])

    if n < rows:
        position = jnp.concatenate([position, jnp.zeros((rows - n, rows), F32)], axis=0)
    post[...] = position.T

    pl.semaphore_wait(stage_sem.at[1], within(stages[2]))
    send_between(stages[0] + stages[1], n)
    for g in range(1, len(parts)):
        for step in range(1, half):
            forward(own + lax.rem(me + step, half), g).start()

    for j in range(n):
        column = jnp.broadcast_to(post[:, j : j + 1], (rows, 128))
        slot_col[:, near(j)] = column.reshape(tiles, TILE, 128)
    for a in range(tiles):
        slot_row[a] = slot_col[a].reshape(tokens, 128).T[0:8, :]

    w = w_buf[...]
    blank = jnp.zeros_like(w)
    wq[...] = jnp.concatenate([w, blank], axis=0)
    wkt[...] = jnp.concatenate([blank, w], axis=0).astype(F32).T.astype(BF16)
    gains = gain_buf[...].astype(F32).reshape(1, n * width)
    gain = jnp.zeros((1, width), F32)
    for h in range(n):
        gain = gain + jnp.where(me == h, gains[:, h * width : (h + 1) * width], 0.0)

    def feature(z):
        return jnp.where(z > 0.0, z + 1.0, jnp.exp(jnp.minimum(z, 0.0))).astype(BF16)

    share = tokens // 2

    def take(a, part):
        g = next(i for i, (first, last) in enumerate(parts) if first <= a < last)
        first = parts[g][0]
        base, mid, _ = starts[g]
        here = slice(base + (a - first) * TILE, base + (a - first + 1) * TILE)
        group = slice(part * half, (part + 1) * half)
        slots = slice(a * tokens + part * share, a * tokens + (part + 1) * share)
        x = recv[group, here, :].reshape(share, 2 * width)
        phi_q[slots, :] = feature(jnp.dot(x, wq[...], preferred_element_type=F32))
        keys = lax.dot_general(wkt[...], x, (((1,), (1,)), ((), ())), preferred_element_type=F32)
        phi_kt[:, slots] = feature(keys)
        there = mid + (a - first) // 2 * TILE
        v = recv[group, there : there + TILE, :].reshape(share, 2 * width)
        val[slots, :] = v[:, width:] if a % 2 else v[:, :width]

    def tile(a, count, b0, b1):
        size = count * tokens
        span = (b1 - b0) * tokens
        scores = jnp.dot(
            phi_q[a * tokens : a * tokens + size, :],
            phi_kt[:, b0 * tokens : b1 * tokens],
            preferred_element_type=F32,
        )
        later = slot_col[a : a + count].reshape(size // 8, 8, 128)
        later = jnp.concatenate([later] * (span // 128), axis=2)
        earlier = jnp.concatenate([slot_row[b] for b in range(b0, b1)], axis=1)
        keep = earlier[None] <= later
        scores = jnp.where(keep, scores.reshape(size // 8, 8, span), 0.0).reshape(size, span)
        high = scores.astype(BF16)
        low = (scores - high.astype(F32)).astype(BF16)
        both = jnp.dot(
            jnp.concatenate([high, low], axis=0),
            val[b0 * tokens : b1 * tokens, :],
            preferred_element_type=F32,
        )
        return both[:size] + both[size:]

    marks = sorted(set(f for f in full if f))

    sums = []

    def add_state():
        b0 = marks[len(sums) - 1] if sums else 0
        b1 = marks[len(sums)]
        total = jnp.dot(
            phi_kt[:, b0 * tokens : b1 * tokens],
            val[b0 * tokens : b1 * tokens, :],
            preferred_element_type=F32,
        )
        if sums:
            total = sums[-1] + total
        high = total.astype(BF16)
        low = (total - high.astype(F32)).astype(BF16)
        state[len(sums)] = jnp.concatenate([high, low], axis=1)
        sums.append(total)

    def from_state(a):
        while len(sums) <= marks.index(full[a]):
            add_state()
        both = jnp.dot(
            phi_q[a * tokens : (a + 1) * tokens, :], state[marks.index(full[a])], preferred_element_type=F32
        )
        return both[:, :width] + both[:, width:]

    def sweep(a, count, b0, b1, step):
        total = None
        for b in range(b0, b1, step):
            piece = tile(a, count, b, min(b + step, b1))
            total = piece if total is None else total + piece
        return total

    def normalise(attended):
        centre = jnp.mean(attended, axis=1, keepdims=True)
        centred = attended - centre
        spread = jnp.mean(centred * centred, axis=1, keepdims=True)
        return (centred * lax.rsqrt(spread + 1e-05) * gain).astype(BF16)

    def pack(a, even, odd):
        y = jnp.concatenate([even, odd], axis=1).reshape(n, TILE, 2 * width)
        out_send[:, a * TILE // 2 : a * TILE // 2 + TILE, :] = y

    def piece_of(g):
        return slice(returns[g][0] * TILE // 2, returns[g][1] * TILE // 2)

    def back(loader, g):
        return pltpu.make_async_remote_copy(
            src_ref=out_send.at[near(loader), piece_of(g)],
            dst_ref=out_recv.at[me, piece_of(g)],
            send_sem=back_send_sem.at[loader, g],
            recv_sem=back_recv_sem.at[me, g],
            device_id={"seq": loader},
            device_id_type=MESH,
        )

    def collect(src, g):
        pltpu.make_async_remote_copy(
            src_ref=out_send.at[src, piece_of(g)],
            dst_ref=out_recv.at[src, piece_of(g)],
            send_sem=back_send_sem.at[src, g],
            recv_sem=back_recv_sem.at[src, g],
            device_id={"seq": src},
            device_id_type=MESH,
        ).wait_recv()

    for g, (first, last) in enumerate(parts):
        for step in range(1, half):
            arrive(own + lax.rem(me + step, half), g)
        for a in range(first, last):
            take(a, 0)

    sent = 0
    done = {}
    for g, (first, last) in enumerate(parts):
        def cross(i, carry):
            peer = lax.rem(own + half + lax.rem(me + i, half), n)
            arrive(peer, g)
            return carry

        for i in range(half):
            cross(i, 0)
        if g + 1 < len(parts):
            def onward(i, carry):
                forward(lax.rem(own + half + lax.rem(me + i, half), n), g + 1).start()
                return carry

            for i in range(half):
                onward(i, 0)
        for b in range(first, last):
            take(b, 1)
        for a in range(last):
            if a < first and ends[a] <= first:
                continue
            total = sweep(a, 1, max(full[a], first if a < first else 0), min(ends[a], last), 3)
            if a < first:
                total = total + acc[a]
            elif full[a]:
                total = total + from_state(a)
            if ends[a] > last:
                acc[a] = total
                continue
            done[a] = normalise(total)
            if a % 2:
                pack(a - 1, done.pop(a - 1), done.pop(a))
            while sent < len(returns) and returns[sent][1] <= a + 1 and a % 2:
                every(ahead, lambda loader: back(loader, sent).start())
                sent += 1
        while len(sums) < len(marks) and marks[len(sums)] <= last:
            add_state()

    out_recv[me] = out_send[near(me)]
    def drain(peer):
        for g in range(len(parts)):
            forward(peer, g).wait_send()
        for g in range(len(returns)):
            back(peer, g).wait_send()

    every(ahead, drain)
    for g, (first, last) in enumerate(returns):
        every(behind, lambda src: collect(src, g))
        for a in range(first, last, 2):
            here = slice(a * TILE // 2, a * TILE // 2 + TILE)
            for pair in range(n // 2):
                lanes = slice(2 * width * pair, 2 * width * (pair + 1))
                x = out_recv[2 * pair, here, :]
                y = out_recv[2 * pair + 1, here, :]
                out_ref[a * TILE : (a + 1) * TILE, lanes] = jnp.concatenate(
                    [x[:, :width], y[:, :width]], axis=1
                )
                out_ref[(a + 1) * TILE : (a + 2) * TILE, lanes] = jnp.concatenate(
                    [x[:, width:], y[:, width:]], axis=1
                )


def grouped_kernel(
    n,
    heads,
    q_ref,
    k_ref,
    v_ref,
    w_ref,
    gain_ref,
    counts_ref,
    offsets_ref,
    out_ref,
    q_buf,
    k_buf,
    v_buf,
    w_buf,
    gain_buf,
    counts_buf,
    offsets_buf,
    load_sem,
    send,
    recv,
    phi_q,
    phi_kt,
    val,
    posr,
    post,
    posc,
    slot_row,
    slot_col,
    acc,
    wq,
    wkt,
    out_send,
    out_recv,
    send_sem,
    recv_sem,
    back_send_sem,
    back_recv_sem,
):
    rows = q_ref.shape[0]
    half = rows // 2
    width = q_ref.shape[1] // heads
    feat = w_ref.shape[2]
    group = n // heads
    part_rows = rows // group
    part_half = part_rows // 2
    total = n * rows
    queries = n * part_rows
    me = lax.axis_index("seq")
    head = me // group
    part = me % group

    half_ring = n // 2
    own = me // half_ring * half_ring
    other = lax.rem(own + half_ring, n)

    def target(step):
        return jnp.where(step < half_ring, own, other) + lax.rem(me + step, half_ring)

    def source(step):
        return jnp.where(step < half_ring, own, other) + lax.rem(me + n - step, half_ring)

    loads = [
        pltpu.make_async_copy(src, dst, load_sem.at[i])
        for i, (src, dst) in enumerate(
            (
                (q_ref, q_buf),
                (k_ref, k_buf),
                (v_ref, v_buf),
                (counts_ref, counts_buf),
                (offsets_ref, offsets_buf),
                (w_ref.at[head], w_buf),
                (gain_ref, gain_buf),
            )
        )
    ]
    for load in loads:
        load.start()

    barrier = pltpu.get_barrier_semaphore()

    def greet(step, carry):
        peer = lax.rem(me + step, n)
        pl.semaphore_signal(barrier, inc=1, device_id={"seq": peer}, device_id_type=MESH)
        return carry

    lax.fori_loop(1, n, greet, 0)

    for load in loads[:3]:
        load.wait()

    for pair in range(heads // 2):
        lanes = slice(2 * width * pair, 2 * width * (pair + 1))
        q = q_buf[:, lanes]
        k = k_buf[:, lanes]
        v = v_buf[:, lanes]
        send[2 * pair, 0:rows, :] = jnp.concatenate([q[:, :width], k[:, :width]], axis=1)
        send[2 * pair + 1, 0:rows, :] = jnp.concatenate([q[:, width:], k[:, width:]], axis=1)
        send[2 * pair, rows:, :] = jnp.concatenate([v[:half, :width], v[half:, :width]], axis=1)
        send[2 * pair + 1, rows:, :] = jnp.concatenate([v[:half, width:], v[half:, width:]], axis=1)

    pl.semaphore_wait(barrier, n - 1)

    def forward(peer):
        return pltpu.make_async_remote_copy(
            src_ref=send.at[peer // group],
            dst_ref=recv.at[me],
            send_sem=send_sem.at[peer],
            recv_sem=recv_sem.at[me],
            device_id={"seq": peer},
            device_id_type=MESH,
        )

    def send_one(step, carry):
        forward(target(step)).start()
        return carry

    lax.fori_loop(1, n, send_one, 0)
    recv[me] = send[head]

    for load in loads[3:]:
        load.wait()

    lane = lax.broadcasted_iota(jnp.int32, (n, rows), 1)
    start = jnp.zeros((n, 1), jnp.int32)
    position = lane
    for d in range(n):
        count = counts_buf[:, d : d + 1]
        inside = (lane >= start) & (lane < start + count)
        position = position + jnp.where(inside, d * rows + offsets_buf[:, d : d + 1] - start, 0)
        start = start + count
    position = position.astype(F32)
    posr[...] = position
    if n < rows:
        position = jnp.concatenate([position, jnp.zeros((rows - n, rows), F32)], axis=0)
    post[...] = position.T
    mine = post[pl.ds(pl.multiple_of(part * part_rows, part_rows), part_rows), :]
    for j in range(n):
        posc[j * part_rows : (j + 1) * part_rows, :] = jnp.broadcast_to(
            mine[:, j : j + 1], (part_rows, 128)
        )

    w = w_buf[...]
    blank = jnp.zeros_like(w)
    wq[...] = jnp.concatenate([w, blank], axis=0)
    wkt[...] = jnp.concatenate([blank, w], axis=0).astype(F32).T.astype(BF16)
    gain = jnp.zeros((1, width), F32)
    for h in range(heads):
        gain = gain + jnp.where(head == h, gain_buf[:, h * width : (h + 1) * width].astype(F32), 0.0)

    def feature(z):
        return jnp.where(z > 0.0, z + 1.0, jnp.exp(jnp.minimum(z, 0.0))).astype(BF16)

    def take_block(step):
        src = source(step)
        x = recv[src, 0:rows, :]
        keys = lax.dot_general(wkt[...], x, (((1,), (1,)), ((), ())), preferred_element_type=F32)
        phi_kt[:, step * rows : (step + 1) * rows] = feature(keys)
        mine_of = pl.multiple_of(part * part_rows, part_rows)
        proj = jnp.dot(
            recv[src, pl.ds(mine_of, part_rows), :], wq[...], preferred_element_type=F32
        )
        slots = slice(step * part_rows, (step + 1) * part_rows)
        phi_q[slots, :] = feature(proj)
        block = recv[src, rows:, :]
        val[step * rows : step * rows + half, :] = block[:, :width]
        val[step * rows + half : (step + 1) * rows, :] = block[:, width:]
        slot_row[step : step + 1, :] = posr[pl.ds(src, 1), :]
        slot_col[slots, :] = posc[
            pl.ds(pl.multiple_of(src * part_rows, part_rows), part_rows), :
        ]

    def arrive(step):
        src = source(step)
        pltpu.make_async_remote_copy(
            src_ref=send.at[0],
            dst_ref=recv.at[src],
            send_sem=send_sem.at[src],
            recv_sem=recv_sem.at[src],
            device_id={"seq": src},
            device_id_type=MESH,
        ).wait_recv()

    groups = min(GROUPS, n)
    per = n // groups
    tile_r = per * part_rows
    tile_s = per * rows

    def tile(rb, sb):
        r0 = pl.multiple_of(rb * tile_r, tile_r)
        s0 = pl.multiple_of(sb * tile_s, tile_s)
        scores = jnp.dot(
            phi_q[pl.ds(r0, tile_r), :], phi_kt[:, pl.ds(s0, tile_s)], preferred_element_type=F32
        )
        later = jnp.concatenate([slot_col[pl.ds(r0, tile_r), :]] * per, axis=1)
        earlier = jnp.concatenate([slot_row[pl.ds(sb * per + i, 1), :] for i in range(per)], axis=1)
        scores = jnp.where(earlier <= later, scores, 0.0)
        high = scores.astype(BF16)
        low = (scores - high.astype(F32)).astype(BF16)
        vals = val[pl.ds(s0, tile_s), :]
        return jnp.dot(high, vals, preferred_element_type=F32) + jnp.dot(
            low, vals, preferred_element_type=F32
        )

    def back(step):
        loader = source(step)
        return pltpu.make_async_remote_copy(
            src_ref=out_send.at[step],
            dst_ref=out_recv.at[me],
            send_sem=back_send_sem.at[loader],
            recv_sem=back_recv_sem.at[me],
            device_id={"seq": loader},
            device_id_type=MESH,
        )

    def finish(rb, attended):
        centre = jnp.mean(attended, axis=1, keepdims=True)
        centred = attended - centre
        spread = jnp.mean(centred * centred, axis=1, keepdims=True)
        normed = (centred * lax.rsqrt(spread + 1e-05) * gain).astype(BF16)
        for i in range(per):
            y = normed[i * part_rows : (i + 1) * part_rows]
            out_send[rb * per + i] = jnp.concatenate([y[:part_half], y[part_half:]], axis=1)
        for i in range(per):
            if rb * per + i > 0:
                back(rb * per + i).start()

    def rows_of(rb):
        return pl.ds(pl.multiple_of(rb * tile_r, tile_r), tile_r)

    for gi in range(groups):
        for step in range(gi * per, (gi + 1) * per):
            if step > 0:
                arrive(step)
            take_block(step)
        last = gi == groups - 1
        fresh = tile(gi, gi)
        if not last:

            def both(i, fresh):
                acc[rows_of(i), :] = acc[rows_of(i), :] + tile(i, gi)
                return fresh + tile(gi, i)

            acc[rows_of(gi), :] = lax.fori_loop(0, gi, both, fresh)
        else:
            finish(gi, lax.fori_loop(0, gi, lambda i, fresh: fresh + tile(gi, i), fresh))
            for i in reversed(range(gi)):
                finish(i, acc[rows_of(i), :] + tile(i, gi))
    out_recv[me] = out_send[0]

    def collect(step, carry):
        src = source(step)
        pltpu.make_async_remote_copy(
            src_ref=out_send.at[step],
            dst_ref=out_recv.at[src],
            send_sem=back_send_sem.at[src],
            recv_sem=back_recv_sem.at[src],
            device_id={"seq": src},
            device_id_type=MESH,
        ).wait_recv()
        return carry

    lax.fori_loop(1, n, collect, 0)

    for piece in range(group):
        first = slice(piece * part_rows, piece * part_rows + part_half)
        second = slice(piece * part_rows + part_half, (piece + 1) * part_rows)
        for pair in range(heads // 2):
            lanes = slice(2 * width * pair, 2 * width * (pair + 1))
            a = out_recv[2 * pair * group + piece]
            b = out_recv[(2 * pair + 1) * group + piece]
            out_ref[first, lanes] = jnp.concatenate([a[:, :width], b[:, :width]], axis=1)
            out_ref[second, lanes] = jnp.concatenate([a[:, width:], b[:, width:]], axis=1)

    def drain(step, carry):
        peer = target(step)
        forward(peer).wait_send()
        back(step).wait_send()
        return carry

    lax.fori_loop(1, n, drain, 0)


def grouped(n, queries, keys, values, feat_weight, norm_gain, counts, offsets):
    rows = queries.shape[0]
    heads, width, feat = feat_weight.shape
    group = n // heads
    part_rows = rows // group
    total = n * rows
    lanes = 2 * width
    return pl.pallas_call(
        functools.partial(grouped_kernel, n, heads),
        out_shape=jax.ShapeDtypeStruct(queries.shape, BF16),
        in_specs=[pl.BlockSpec(memory_space=pltpu.HBM)] * 7,
        out_specs=pl.BlockSpec(memory_space=pltpu.VMEM),
        scratch_shapes=[
            pltpu.VMEM(queries.shape, BF16),
            pltpu.VMEM(keys.shape, BF16),
            pltpu.VMEM(values.shape, BF16),
            pltpu.VMEM((width, feat), BF16),
            pltpu.VMEM((1, norm_gain.shape[0]), BF16),
            pltpu.VMEM(counts.shape, jnp.int32),
            pltpu.VMEM(offsets.shape, jnp.int32),
            pltpu.SemaphoreType.DMA((7,)),
            pltpu.VMEM((heads, rows + rows // 2, lanes), BF16),
            pltpu.VMEM((n, rows + rows // 2, lanes), BF16),
            pltpu.VMEM((n * part_rows, feat), BF16),
            pltpu.VMEM((feat, total), BF16),
            pltpu.VMEM((total, width), BF16),
            pltpu.VMEM((n, rows), F32),
            pltpu.VMEM((rows, max(n, rows)), F32),
            pltpu.VMEM((n * part_rows, 128), F32),
            pltpu.VMEM((n, rows), F32),
            pltpu.VMEM((n * part_rows, 128), F32),
            pltpu.VMEM((n * part_rows, width), F32),
            pltpu.VMEM((lanes, feat), BF16),
            pltpu.VMEM((feat, lanes), BF16),
            pltpu.VMEM((n, part_rows // 2, lanes), BF16),
            pltpu.VMEM((n, part_rows // 2, lanes), BF16),
            pltpu.SemaphoreType.DMA((n,)),
            pltpu.SemaphoreType.DMA((n,)),
            pltpu.SemaphoreType.DMA((n,)),
            pltpu.SemaphoreType.DMA((n,)),
        ],
        compiler_params=pltpu.CompilerParams(
            collective_id=0, has_side_effects=True, vmem_limit_bytes=67043328
        ),
    )(queries, keys, values, feat_weight, norm_gain.reshape(1, -1), counts, offsets)

def per_device(n, queries, keys, values, feat_weight, norm_gain, counts, offsets):
    rows = queries.shape[0]
    heads, width, feat = feat_weight.shape
    if n != heads or n % 4 or n > rows or rows % (8 * TILE):
        return grouped(n, queries, keys, values, feat_weight, norm_gain, counts, offsets)
    lanes = 2 * width
    tiles = rows // TILE
    tokens = n * TILE
    total = n * rows
    cut = tiles * 3 // 4
    parts = ((0, cut), (cut, tiles))
    returns = ((0, 2), (2, tiles))
    return pl.pallas_call(
        functools.partial(kernel, n, parts, returns),
        out_shape=pltpu.VMEM(queries.shape, BF16),
        in_specs=[pl.BlockSpec(memory_space=pltpu.HBM)] * 7,
        out_specs=pl.BlockSpec(memory_space=pltpu.VMEM),
        scratch_shapes=[
            pltpu.VMEM(queries.shape, BF16),
            pltpu.VMEM(keys.shape, BF16),
            pltpu.VMEM(values.shape, BF16),
            pltpu.VMEM((width, feat), BF16),
            pltpu.VMEM(norm_gain.shape, BF16),
            pltpu.VMEM(counts.shape, jnp.int32),
            pltpu.VMEM(offsets.shape, jnp.int32),
            pltpu.SemaphoreType.DMA((7,)),
            pltpu.VMEM((n, rows + rows // 2, lanes), BF16),
            pltpu.VMEM((n, rows + rows // 2, lanes), BF16),
            pltpu.VMEM((total, feat), BF16),
            pltpu.VMEM((feat, total), BF16),
            pltpu.VMEM((total, width), BF16),
            pltpu.VMEM((rows, max(n, rows)), F32),
            pltpu.VMEM((tiles, 8, tokens), F32),
            pltpu.VMEM((tiles, n, TILE, 128), F32),
            pltpu.VMEM((tiles, tokens, width), F32),
            pltpu.VMEM((tiles, feat, lanes), BF16),
            pltpu.VMEM((lanes, feat), BF16),
            pltpu.VMEM((feat, lanes), BF16),
            pltpu.VMEM((n, rows // 2, lanes), BF16),
            pltpu.VMEM((n, rows // 2, lanes), BF16),
            pltpu.SemaphoreType.DMA((n, len(parts))),
            pltpu.SemaphoreType.DMA((n, len(parts))),
            pltpu.SemaphoreType.DMA((n, len(returns))),
            pltpu.SemaphoreType.DMA((n, len(returns))),
            pltpu.SemaphoreType.REGULAR((2,)),
        ],
        compiler_params=pltpu.CompilerParams(
            collective_id=0, has_side_effects=True, vmem_limit_bytes=60000000
        ),
    )(queries, keys, values, feat_weight, norm_gain, counts, offsets)


def solution(mesh):
    in_specs = (
        P(("dp", "seq"), None),
        P(("dp", "seq"), None),
        P(("dp", "seq"), None),
        P(),
        P(),
        P("dp", None),
        P("dp", None),
    )
    return jax.shard_map(
        functools.partial(per_device, mesh.shape["seq"]),
        mesh=mesh,
        in_specs=in_specs,
        out_specs=P(("dp", "seq"), None),
        check_vma=False,
    )
```

```python
import functools

import jax
import jax.numpy as jnp
from jax import lax
from jax.experimental import pallas as pl
from jax.experimental.pallas import tpu as pltpu
from jax.sharding import PartitionSpec as P

MESH = pl.DeviceIdType.MESH
F32 = jnp.float32
BF16 = jnp.bfloat16
GROUPS = 4
TILE = 16


def block_bounds(n, rows, i):
    least = rows // n // 2
    most = 3 * (rows // n) // 2
    first = min(d for d in range(n) if min(most * (d + 1), rows - least * (n - d - 1)) > i)
    last = max(d for d in range(n) if max(least * d, rows - most * (n - d)) <= i)
    return first, last


def kernel(
    n,
    parts,
    returns,
    q_ref,
    k_ref,
    v_ref,
    w_ref,
    gain_ref,
    counts_ref,
    offsets_ref,
    out_ref,
    q_buf,
    k_buf,
    v_buf,
    w_buf,
    gain_buf,
    counts_buf,
    offsets_buf,
    load_sem,
    send,
    recv,
    phi_q,
    phi_kt,
    val,
    post,
    slot_row,
    slot_col,
    acc,
    state,
    wq,
    wkt,
    out_send,
    out_recv,
    send_sem,
    recv_sem,
    back_send_sem,
    back_recv_sem,
    stage_sem,
):
    rows = q_ref.shape[0]
    width = q_ref.shape[1] // n
    tiles = rows // TILE
    tokens = n * TILE
    me = lax.axis_index("seq")

    bounds = [
        (block_bounds(n, rows, TILE * a)[0], block_bounds(n, rows, TILE * a + TILE - 1)[1])
        for a in range(tiles)
    ]
    full = [sum(1 for b in range(tiles) if bounds[b][1] < bounds[a][0]) for a in range(tiles)]
    ends = [sum(1 for b in range(tiles) if bounds[b][0] <= bounds[a][1]) for a in range(tiles)]

    half = n // 2
    own = me // half * half

    def near(dev):
        return lax.rem(dev + n - own, n)

    def near_for(peer):
        return lax.rem(me + n - peer // half * half, n)

    loads = [
        pltpu.make_async_copy(src, dst, load_sem.at[i])
        for i, (src, dst) in enumerate(
            (
                (q_ref, q_buf),
                (k_ref, k_buf),
                (v_ref, v_buf),
                (counts_ref, counts_buf),
                (offsets_ref, offsets_buf),
                (w_ref.at[me], w_buf),
                (gain_ref, gain_buf),
            )
        )
    ]
    for load in loads:
        load.start()

    def hops(peer):
        across = jnp.abs(peer // 4 - me // 4)
        return across + jnp.abs(peer // 2 % 2 - me // 2 % 2)

    def each(order, do):
        def body(step, carry):
            do(order(step))
            return carry

        lax.fori_loop(1, n, body, 0)

    def every(order, do):
        for step in range(1, n):
            do(order(step))

    def swap(step):
        return me ^ step

    def ahead(step):
        return lax.rem(me + step, n)

    def behind(step):
        return lax.rem(me + n - step, n)

    def tell(sem, reach):
        def one(peer):
            @pl.when(hops(peer) <= reach)
            def _():
                pl.semaphore_signal(sem, inc=1, device_id={"seq": peer}, device_id_type=MESH)

        each(swap, one)

    def within(reach):
        return sum(jnp.where(hops(me ^ step) <= reach, 1, 0) for step in range(1, n))

    stages = [1, 1, max(n // 4 - 2, 1)]
    barrier = pltpu.get_barrier_semaphore()
    tell(barrier, stages[0])

    for load in loads[:3]:
        load.wait()

    starts = []
    at = 0
    for first, last in parts:
        starts.append((at, at + (last - first) * TILE, at + (last - first) * (TILE + TILE // 2)))
        at = starts[-1][2]

    for pair in range(n // 2):
        lanes = slice(2 * width * pair, 2 * width * (pair + 1))
        q = q_buf[:, lanes]
        k = k_buf[:, lanes]
        v = v_buf[:, lanes]
        for (first, last), (base, mid, end) in zip(parts, starts):
            here = slice(first * TILE, last * TILE)
            send[2 * pair, base:mid, :] = jnp.concatenate([q[here, :width], k[here, :width]], axis=1)
            send[2 * pair + 1, base:mid, :] = jnp.concatenate([q[here, width:], k[here, width:]], axis=1)
            for a in range(first, last, 2):
                to = slice(mid + (a - first) * TILE // 2, mid + (a - first + 2) * TILE // 2)
                even = v[a * TILE : (a + 1) * TILE]
                odd = v[(a + 1) * TILE : (a + 2) * TILE]
                send[2 * pair, to, :] = jnp.concatenate([even[:, :width], odd[:, :width]], axis=1)
                send[2 * pair + 1, to, :] = jnp.concatenate([even[:, width:], odd[:, width:]], axis=1)

    def forward(peer, g):
        piece = slice(starts[g][0], starts[g][2])
        return pltpu.make_async_remote_copy(
            src_ref=send.at[peer, piece],
            dst_ref=recv.at[near_for(peer), piece],
            send_sem=send_sem.at[peer, g],
            recv_sem=recv_sem.at[me, g],
            device_id={"seq": peer},
            device_id_type=MESH,
        )

    def arrive(src, g):
        piece = slice(starts[g][0], starts[g][2])
        pltpu.make_async_remote_copy(
            src_ref=send.at[src, piece],
            dst_ref=recv.at[near(src), piece],
            send_sem=send_sem.at[src, g],
            recv_sem=recv_sem.at[src, g],
            device_id={"seq": src},
            device_id_type=MESH,
        ).wait_recv()

    def send_between(low, high):
        def one(peer):
            @pl.when((hops(peer) > low) & (hops(peer) <= high))
            def _():
                forward(peer, 0).start()

        each(swap, one)

    pl.semaphore_wait(barrier, within(stages[0]))
    tell(stage_sem.at[0], stages[1])
    send_between(-1, stages[0])
    recv[near(me)] = send[me]

    for load in loads[3:]:
        load.wait()
    lane = lax.broadcasted_iota(jnp.int32, (n, rows), 1)
    start = jnp.zeros((n, 1), jnp.int32)
    position = lane
    for d in range(n):
        count = counts_buf[:, d : d + 1]
        inside = (lane >= start) & (lane < start + count)
        position = position + jnp.where(inside, d * rows + offsets_buf[:, d : d + 1] - start, 0)
        start = start + count
    position = position.astype(F32)

    pl.semaphore_wait(stage_sem.at[0], within(stages[1]))
    tell(stage_sem.at[1], stages[2])
    send_between(stages[0], stages[0] + stages[1])

    if n < rows:
        position = jnp.concatenate([position, jnp.zeros((rows - n, rows), F32)], axis=0)
    post[...] = position.T

    pl.semaphore_wait(stage_sem.at[1], within(stages[2]))
    send_between(stages[0] + stages[1], n)
    for g in range(1, len(parts)):
        for step in range(1, half):
            forward(own + lax.rem(me + step, half), g).start()

    for j in range(n):
        column = jnp.broadcast_to(post[:, j : j + 1], (rows, 128))
        slot_col[:, near(j)] = column.reshape(tiles, TILE, 128)
    for a in range(tiles):
        slot_row[a] = slot_col[a].reshape(tokens, 128).T[0:8, :]

    w = w_buf[...]
    blank = jnp.zeros_like(w)
    wq[...] = jnp.concatenate([w, blank], axis=0)
    wkt[...] = jnp.concatenate([blank, w], axis=0).astype(F32).T.astype(BF16)
    gains = gain_buf[...].astype(F32).reshape(1, n * width)
    gain = jnp.zeros((1, width), F32)
    for h in range(n):
        gain = gain + jnp.where(me == h, gains[:, h * width : (h + 1) * width], 0.0)

    def feature(z):
        return jnp.where(z > 0.0, z + 1.0, jnp.exp(jnp.minimum(z, 0.0))).astype(BF16)

    share = tokens // 2

    def take(a, part):
        g = next(i for i, (first, last) in enumerate(parts) if first <= a < last)
        first = parts[g][0]
        base, mid, _ = starts[g]
        here = slice(base + (a - first) * TILE, base + (a - first + 1) * TILE)
        group = slice(part * half, (part + 1) * half)
        slots = slice(a * tokens + part * share, a * tokens + (part + 1) * share)
        x = recv[group, here, :].reshape(share, 2 * width)
        phi_q[slots, :] = feature(jnp.dot(x, wq[...], preferred_element_type=F32))
        keys = lax.dot_general(wkt[...], x, (((1,), (1,)), ((), ())), preferred_element_type=F32)
        phi_kt[:, slots] = feature(keys)
        there = mid + (a - first) // 2 * TILE
        v = recv[group, there : there + TILE, :].reshape(share, 2 * width)
        val[slots, :] = v[:, width:] if a % 2 else v[:, :width]

    def tile(a, count, b0, b1):
        size = count * tokens
        span = (b1 - b0) * tokens
        scores = jnp.dot(
            phi_q[a * tokens : a * tokens + size, :],
            phi_kt[:, b0 * tokens : b1 * tokens],
            preferred_element_type=F32,
        )
        later = slot_col[a : a + count].reshape(size // 8, 8, 128)
        later = jnp.concatenate([later] * (span // 128), axis=2)
        earlier = jnp.concatenate([slot_row[b] for b in range(b0, b1)], axis=1)
        keep = earlier[None] <= later
        scores = jnp.where(keep, scores.reshape(size // 8, 8, span), 0.0).reshape(size, span)
        high = scores.astype(BF16)
        low = (scores - high.astype(F32)).astype(BF16)
        both = jnp.dot(
            jnp.concatenate([high, low], axis=0),
            val[b0 * tokens : b1 * tokens, :],
            preferred_element_type=F32,
        )
        return both[:size] + both[size:]

    marks = sorted(set(f for f in full if f))

    sums = []

    def add_state():
        b0 = marks[len(sums) - 1] if sums else 0
        b1 = marks[len(sums)]
        total = jnp.dot(
            phi_kt[:, b0 * tokens : b1 * tokens],
            val[b0 * tokens : b1 * tokens, :],
            preferred_element_type=F32,
        )
        if sums:
            total = sums[-1] + total
        high = total.astype(BF16)
        low = (total - high.astype(F32)).astype(BF16)
        state[len(sums)] = jnp.concatenate([high, low], axis=1)
        sums.append(total)

    def from_state(a):
        while len(sums) <= marks.index(full[a]):
            add_state()
        both = jnp.dot(
            phi_q[a * tokens : (a + 1) * tokens, :], state[marks.index(full[a])], preferred_element_type=F32
        )
        return both[:, :width] + both[:, width:]

    def sweep(a, count, b0, b1, step):
        total = None
        for b in range(b0, b1, step):
            piece = tile(a, count, b, min(b + step, b1))
            total = piece if total is None else total + piece
        return total

    def normalise(attended):
        centre = jnp.mean(attended, axis=1, keepdims=True)
        centred = attended - centre
        spread = jnp.mean(centred * centred, axis=1, keepdims=True)
        return (centred * lax.rsqrt(spread + 1e-05) * gain).astype(BF16)

    def pack(a, even, odd):
        y = jnp.concatenate([even, odd], axis=1).reshape(n, TILE, 2 * width)
        out_send[:, a * TILE // 2 : a * TILE // 2 + TILE, :] = y

    def piece_of(g):
        return slice(returns[g][0] * TILE // 2, returns[g][1] * TILE // 2)

    def back(loader, g):
        return pltpu.make_async_remote_copy(
            src_ref=out_send.at[near(loader), piece_of(g)],
            dst_ref=out_recv.at[me, piece_of(g)],
            send_sem=back_send_sem.at[loader, g],
            recv_sem=back_recv_sem.at[me, g],
            device_id={"seq": loader},
            device_id_type=MESH,
        )

    def collect(src, g):
        pltpu.make_async_remote_copy(
            src_ref=out_send.at[src, piece_of(g)],
            dst_ref=out_recv.at[src, piece_of(g)],
            send_sem=back_send_sem.at[src, g],
            recv_sem=back_recv_sem.at[src, g],
            device_id={"seq": src},
            device_id_type=MESH,
        ).wait_recv()

    for g, (first, last) in enumerate(parts):
        for step in range(1, half):
            arrive(own + lax.rem(me + step, half), g)
        for a in range(first, last):
            take(a, 0)

    sent = 0
    done = {}
    for g, (first, last) in enumerate(parts):
        def cross(i, carry):
            peer = lax.rem(own + half + lax.rem(me + i, half), n)
            arrive(peer, g)
            return carry

        for i in range(half):
            cross(i, 0)
        if g + 1 < len(parts):
            def onward(i, carry):
                forward(lax.rem(own + half + lax.rem(me + i + 1, half), n), g + 1).start()
                return carry

            for i in range(half):
                onward(i, 0)
        for b in range(first, last):
            take(b, 1)
        for a in range(last):
            if a < first and ends[a] <= first:
                continue
            total = sweep(a, 1, max(full[a], first if a < first else 0), min(ends[a], last), 3)
            if a < first:
                total = total + acc[a]
            elif full[a]:
                total = total + from_state(a)
            if ends[a] > last:
                acc[a] = total
                continue
            done[a] = normalise(total)
            if a % 2:
                pack(a - 1, done.pop(a - 1), done.pop(a))
            while sent < len(returns) and returns[sent][1] <= a + 1 and a % 2:
                every(ahead, lambda loader: back(loader, sent).start())
                sent += 1
        while len(sums) < len(marks) and marks[len(sums)] <= last:
            add_state()

    out_recv[me] = out_send[near(me)]
    def drain(peer):
        for g in range(len(parts)):
            forward(peer, g).wait_send()
        for g in range(len(returns)):
            back(peer, g).wait_send()

    every(ahead, drain)
    for g, (first, last) in enumerate(returns):
        every(behind, lambda src: collect(src, g))
        for a in range(first, last, 2):
            here = slice(a * TILE // 2, a * TILE // 2 + TILE)
            for pair in range(n // 2):
                lanes = slice(2 * width * pair, 2 * width * (pair + 1))
                x = out_recv[2 * pair, here, :]
                y = out_recv[2 * pair + 1, here, :]
                out_ref[a * TILE : (a + 1) * TILE, lanes] = jnp.concatenate(
                    [x[:, :width], y[:, :width]], axis=1
                )
                out_ref[(a + 1) * TILE : (a + 2) * TILE, lanes] = jnp.concatenate(
                    [x[:, width:], y[:, width:]], axis=1
                )


def grouped_kernel(
    n,
    heads,
    q_ref,
    k_ref,
    v_ref,
    w_ref,
    gain_ref,
    counts_ref,
    offsets_ref,
    out_ref,
    q_buf,
    k_buf,
    v_buf,
    w_buf,
    gain_buf,
    counts_buf,
    offsets_buf,
    load_sem,
    send,
    recv,
    phi_q,
    phi_kt,
    val,
    posr,
    post,
    posc,
    slot_row,
    slot_col,
    acc,
    wq,
    wkt,
    out_send,
    out_recv,
    send_sem,
    recv_sem,
    back_send_sem,
    back_recv_sem,
):
    rows = q_ref.shape[0]
    half = rows // 2
    width = q_ref.shape[1] // heads
    feat = w_ref.shape[2]
    group = n // heads
    part_rows = rows // group
    part_half = part_rows // 2
    total = n * rows
    queries = n * part_rows
    me = lax.axis_index("seq")
    head = me // group
    part = me % group

    half_ring = n // 2
    own = me // half_ring * half_ring
    other = lax.rem(own + half_ring, n)

    def target(step):
        return jnp.where(step < half_ring, own, other) + lax.rem(me + step, half_ring)

    def source(step):
        return jnp.where(step < half_ring, own, other) + lax.rem(me + n - step, half_ring)

    loads = [
        pltpu.make_async_copy(src, dst, load_sem.at[i])
        for i, (src, dst) in enumerate(
            (
                (q_ref, q_buf),
                (k_ref, k_buf),
                (v_ref, v_buf),
                (counts_ref, counts_buf),
                (offsets_ref, offsets_buf),
                (w_ref.at[head], w_buf),
                (gain_ref, gain_buf),
            )
        )
    ]
    for load in loads:
        load.start()

    barrier = pltpu.get_barrier_semaphore()

    def greet(step, carry):
        peer = lax.rem(me + step, n)
        pl.semaphore_signal(barrier, inc=1, device_id={"seq": peer}, device_id_type=MESH)
        return carry

    lax.fori_loop(1, n, greet, 0)

    for load in loads[:3]:
        load.wait()

    for pair in range(heads // 2):
        lanes = slice(2 * width * pair, 2 * width * (pair + 1))
        q = q_buf[:, lanes]
        k = k_buf[:, lanes]
        v = v_buf[:, lanes]
        send[2 * pair, 0:rows, :] = jnp.concatenate([q[:, :width], k[:, :width]], axis=1)
        send[2 * pair + 1, 0:rows, :] = jnp.concatenate([q[:, width:], k[:, width:]], axis=1)
        send[2 * pair, rows:, :] = jnp.concatenate([v[:half, :width], v[half:, :width]], axis=1)
        send[2 * pair + 1, rows:, :] = jnp.concatenate([v[:half, width:], v[half:, width:]], axis=1)

    pl.semaphore_wait(barrier, n - 1)

    def forward(peer):
        return pltpu.make_async_remote_copy(
            src_ref=send.at[peer // group],
            dst_ref=recv.at[me],
            send_sem=send_sem.at[peer],
            recv_sem=recv_sem.at[me],
            device_id={"seq": peer},
            device_id_type=MESH,
        )

    def send_one(step, carry):
        forward(target(step)).start()
        return carry

    lax.fori_loop(1, n, send_one, 0)
    recv[me] = send[head]

    for load in loads[3:]:
        load.wait()

    lane = lax.broadcasted_iota(jnp.int32, (n, rows), 1)
    start = jnp.zeros((n, 1), jnp.int32)
    position = lane
    for d in range(n):
        count = counts_buf[:, d : d + 1]
        inside = (lane >= start) & (lane < start + count)
        position = position + jnp.where(inside, d * rows + offsets_buf[:, d : d + 1] - start, 0)
        start = start + count
    position = position.astype(F32)
    posr[...] = position
    if n < rows:
        position = jnp.concatenate([position, jnp.zeros((rows - n, rows), F32)], axis=0)
    post[...] = position.T
    mine = post[pl.ds(pl.multiple_of(part * part_rows, part_rows), part_rows), :]
    for j in range(n):
        posc[j * part_rows : (j + 1) * part_rows, :] = jnp.broadcast_to(
            mine[:, j : j + 1], (part_rows, 128)
        )

    w = w_buf[...]
    blank = jnp.zeros_like(w)
    wq[...] = jnp.concatenate([w, blank], axis=0)
    wkt[...] = jnp.concatenate([blank, w], axis=0).astype(F32).T.astype(BF16)
    gain = jnp.zeros((1, width), F32)
    for h in range(heads):
        gain = gain + jnp.where(head == h, gain_buf[:, h * width : (h + 1) * width].astype(F32), 0.0)

    def feature(z):
        return jnp.where(z > 0.0, z + 1.0, jnp.exp(jnp.minimum(z, 0.0))).astype(BF16)

    def take_block(step):
        src = source(step)
        x = recv[src, 0:rows, :]
        keys = lax.dot_general(wkt[...], x, (((1,), (1,)), ((), ())), preferred_element_type=F32)
        phi_kt[:, step * rows : (step + 1) * rows] = feature(keys)
        mine_of = pl.multiple_of(part * part_rows, part_rows)
        proj = jnp.dot(
            recv[src, pl.ds(mine_of, part_rows), :], wq[...], preferred_element_type=F32
        )
        slots = slice(step * part_rows, (step + 1) * part_rows)
        phi_q[slots, :] = feature(proj)
        block = recv[src, rows:, :]
        val[step * rows : step * rows + half, :] = block[:, :width]
        val[step * rows + half : (step + 1) * rows, :] = block[:, width:]
        slot_row[step : step + 1, :] = posr[pl.ds(src, 1), :]
        slot_col[slots, :] = posc[
            pl.ds(pl.multiple_of(src * part_rows, part_rows), part_rows), :
        ]

    def arrive(step):
        src = source(step)
        pltpu.make_async_remote_copy(
            src_ref=send.at[0],
            dst_ref=recv.at[src],
            send_sem=send_sem.at[src],
            recv_sem=recv_sem.at[src],
            device_id={"seq": src},
            device_id_type=MESH,
        ).wait_recv()

    groups = min(GROUPS, n)
    per = n // groups
    tile_r = per * part_rows
    tile_s = per * rows

    def tile(rb, sb):
        r0 = pl.multiple_of(rb * tile_r, tile_r)
        s0 = pl.multiple_of(sb * tile_s, tile_s)
        scores = jnp.dot(
            phi_q[pl.ds(r0, tile_r), :], phi_kt[:, pl.ds(s0, tile_s)], preferred_element_type=F32
        )
        later = jnp.concatenate([slot_col[pl.ds(r0, tile_r), :]] * per, axis=1)
        earlier = jnp.concatenate([slot_row[pl.ds(sb * per + i, 1), :] for i in range(per)], axis=1)
        scores = jnp.where(earlier <= later, scores, 0.0)
        high = scores.astype(BF16)
        low = (scores - high.astype(F32)).astype(BF16)
        vals = val[pl.ds(s0, tile_s), :]
        return jnp.dot(high, vals, preferred_element_type=F32) + jnp.dot(
            low, vals, preferred_element_type=F32
        )

    def back(step):
        loader = source(step)
        return pltpu.make_async_remote_copy(
            src_ref=out_send.at[step],
            dst_ref=out_recv.at[me],
            send_sem=back_send_sem.at[loader],
            recv_sem=back_recv_sem.at[me],
            device_id={"seq": loader},
            device_id_type=MESH,
        )

    def finish(rb, attended):
        centre = jnp.mean(attended, axis=1, keepdims=True)
        centred = attended - centre
        spread = jnp.mean(centred * centred, axis=1, keepdims=True)
        normed = (centred * lax.rsqrt(spread + 1e-05) * gain).astype(BF16)
        for i in range(per):
            y = normed[i * part_rows : (i + 1) * part_rows]
            out_send[rb * per + i] = jnp.concatenate([y[:part_half], y[part_half:]], axis=1)
        for i in range(per):
            if rb * per + i > 0:
                back(rb * per + i).start()

    def rows_of(rb):
        return pl.ds(pl.multiple_of(rb * tile_r, tile_r), tile_r)

    for gi in range(groups):
        for step in range(gi * per, (gi + 1) * per):
            if step > 0:
                arrive(step)
            take_block(step)
        last = gi == groups - 1
        fresh = tile(gi, gi)
        if not last:

            def both(i, fresh):
                acc[rows_of(i), :] = acc[rows_of(i), :] + tile(i, gi)
                return fresh + tile(gi, i)

            acc[rows_of(gi), :] = lax.fori_loop(0, gi, both, fresh)
        else:
            finish(gi, lax.fori_loop(0, gi, lambda i, fresh: fresh + tile(gi, i), fresh))
            for i in reversed(range(gi)):
                finish(i, acc[rows_of(i), :] + tile(i, gi))
    out_recv[me] = out_send[0]

    def collect(step, carry):
        src = source(step)
        pltpu.make_async_remote_copy(
            src_ref=out_send.at[step],
            dst_ref=out_recv.at[src],
            send_sem=back_send_sem.at[src],
            recv_sem=back_recv_sem.at[src],
            device_id={"seq": src},
            device_id_type=MESH,
        ).wait_recv()
        return carry

    lax.fori_loop(1, n, collect, 0)

    for piece in range(group):
        first = slice(piece * part_rows, piece * part_rows + part_half)
        second = slice(piece * part_rows + part_half, (piece + 1) * part_rows)
        for pair in range(heads // 2):
            lanes = slice(2 * width * pair, 2 * width * (pair + 1))
            a = out_recv[2 * pair * group + piece]
            b = out_recv[(2 * pair + 1) * group + piece]
            out_ref[first, lanes] = jnp.concatenate([a[:, :width], b[:, :width]], axis=1)
            out_ref[second, lanes] = jnp.concatenate([a[:, width:], b[:, width:]], axis=1)

    def drain(step, carry):
        peer = target(step)
        forward(peer).wait_send()
        back(step).wait_send()
        return carry

    lax.fori_loop(1, n, drain, 0)


def grouped(n, queries, keys, values, feat_weight, norm_gain, counts, offsets):
    rows = queries.shape[0]
    heads, width, feat = feat_weight.shape
    group = n // heads
    part_rows = rows // group
    total = n * rows
    lanes = 2 * width
    return pl.pallas_call(
        functools.partial(grouped_kernel, n, heads),
        out_shape=jax.ShapeDtypeStruct(queries.shape, BF16),
        in_specs=[pl.BlockSpec(memory_space=pltpu.HBM)] * 7,
        out_specs=pl.BlockSpec(memory_space=pltpu.VMEM),
        scratch_shapes=[
            pltpu.VMEM(queries.shape, BF16),
            pltpu.VMEM(keys.shape, BF16),
            pltpu.VMEM(values.shape, BF16),
            pltpu.VMEM((width, feat), BF16),
            pltpu.VMEM((1, norm_gain.shape[0]), BF16),
            pltpu.VMEM(counts.shape, jnp.int32),
            pltpu.VMEM(offsets.shape, jnp.int32),
            pltpu.SemaphoreType.DMA((7,)),
            pltpu.VMEM((heads, rows + rows // 2, lanes), BF16),
            pltpu.VMEM((n, rows + rows // 2, lanes), BF16),
            pltpu.VMEM((n * part_rows, feat), BF16),
            pltpu.VMEM((feat, total), BF16),
            pltpu.VMEM((total, width), BF16),
            pltpu.VMEM((n, rows), F32),
            pltpu.VMEM((rows, max(n, rows)), F32),
            pltpu.VMEM((n * part_rows, 128), F32),
            pltpu.VMEM((n, rows), F32),
            pltpu.VMEM((n * part_rows, 128), F32),
            pltpu.VMEM((n * part_rows, width), F32),
            pltpu.VMEM((lanes, feat), BF16),
            pltpu.VMEM((feat, lanes), BF16),
            pltpu.VMEM((n, part_rows // 2, lanes), BF16),
            pltpu.VMEM((n, part_rows // 2, lanes), BF16),
            pltpu.SemaphoreType.DMA((n,)),
            pltpu.SemaphoreType.DMA((n,)),
            pltpu.SemaphoreType.DMA((n,)),
            pltpu.SemaphoreType.DMA((n,)),
        ],
        compiler_params=pltpu.CompilerParams(
            collective_id=0, has_side_effects=True, vmem_limit_bytes=67043328
        ),
    )(queries, keys, values, feat_weight, norm_gain.reshape(1, -1), counts, offsets)

def per_device(n, queries, keys, values, feat_weight, norm_gain, counts, offsets):
    rows = queries.shape[0]
    heads, width, feat = feat_weight.shape
    if n != heads or n % 4 or n > rows or rows % (8 * TILE):
        return grouped(n, queries, keys, values, feat_weight, norm_gain, counts, offsets)
    lanes = 2 * width
    tiles = rows // TILE
    tokens = n * TILE
    total = n * rows
    cut = tiles * 3 // 4
    parts = ((0, cut), (cut, tiles))
    returns = ((0, 2), (2, tiles))
    return pl.pallas_call(
        functools.partial(kernel, n, parts, returns),
        out_shape=pltpu.VMEM(queries.shape, BF16),
        in_specs=[pl.BlockSpec(memory_space=pltpu.HBM)] * 7,
        out_specs=pl.BlockSpec(memory_space=pltpu.VMEM),
        scratch_shapes=[
            pltpu.VMEM(queries.shape, BF16),
            pltpu.VMEM(keys.shape, BF16),
            pltpu.VMEM(values.shape, BF16),
            pltpu.VMEM((width, feat), BF16),
            pltpu.VMEM(norm_gain.shape, BF16),
            pltpu.VMEM(counts.shape, jnp.int32),
            pltpu.VMEM(offsets.shape, jnp.int32),
            pltpu.SemaphoreType.DMA((7,)),
            pltpu.VMEM((n, rows + rows // 2, lanes), BF16),
            pltpu.VMEM((n, rows + rows // 2, lanes), BF16),
            pltpu.VMEM((total, feat), BF16),
            pltpu.VMEM((feat, total), BF16),
            pltpu.VMEM((total, width), BF16),
            pltpu.VMEM((rows, max(n, rows)), F32),
            pltpu.VMEM((tiles, 8, tokens), F32),
            pltpu.VMEM((tiles, n, TILE, 128), F32),
            pltpu.VMEM((tiles, tokens, width), F32),
            pltpu.VMEM((tiles, feat, lanes), BF16),
            pltpu.VMEM((lanes, feat), BF16),
            pltpu.VMEM((feat, lanes), BF16),
            pltpu.VMEM((n, rows // 2, lanes), BF16),
            pltpu.VMEM((n, rows // 2, lanes), BF16),
            pltpu.SemaphoreType.DMA((n, len(parts))),
            pltpu.SemaphoreType.DMA((n, len(parts))),
            pltpu.SemaphoreType.DMA((n, len(returns))),
            pltpu.SemaphoreType.DMA((n, len(returns))),
            pltpu.SemaphoreType.REGULAR((2,)),
        ],
        compiler_params=pltpu.CompilerParams(
            collective_id=0, has_side_effects=True, vmem_limit_bytes=60000000
        ),
    )(queries, keys, values, feat_weight, norm_gain, counts, offsets)


def solution(mesh):
    in_specs = (
        P(("dp", "seq"), None),
        P(("dp", "seq"), None),
        P(("dp", "seq"), None),
        P(),
        P(),
        P("dp", None),
        P("dp", None),
    )
    return jax.shard_map(
        functools.partial(per_device, mesh.shape["seq"]),
        mesh=mesh,
        in_specs=in_specs,
        out_specs=P(("dp", "seq"), None),
        check_vma=False,
    )
```
